256 devices in a mesh: ep: 32 (over x, z), tp: 8 (over y, core).
Axes of the slice: x: 4, y: 4, z: 8, core: 2. Of those that a mesh axis runs over, the one named last changes fastest.
Arguments:
- attn_out: bfloat16 [8192, 2048], P('ep', 'tp'), may hold values from -6 to 6
- out_proj: bfloat16 [2048, 2048], P('tp'), may hold values from -0.125 to 0.125
- residual: bfloat16 [8192, 2048], P('ep'), may hold values from -40 to 40
- norm_gain: float32 [2048], replicated, may hold values from 0.25 to 1.75
- router: bfloat16 [2048, 64], replicated, may hold values from -0.125 to 0.125
- expert_gate_up: bfloat16 [256, 2, 352, 2048], P(('ep', 'tp')), may hold values from -0.125 to 0.125
- expert_down: bfloat16 [256, 352, 2048], P(('ep', 'tp')), may hold values from -0.15625 to 0.15625
- shared_gate_up: bfloat16 [2, 2816, 2048], P(None, 'tp'), may hold values from -0.125 to 0.125
- shared_down: bfloat16 [2816, 2048], P('tp'), may hold values from -0.109375 to 0.109375
- routes: int32 [8192, 6], P('ep'), may hold values from 0 to 63, all different within a row; in each aligned block of 256 rows (0 to 255, 256 to 511, ...) at most 40 rows name the same one
- live_rows: int32 [32], P('ep'), may hold values from 128 to 256, as said below
- next_gain: float32 [2048], replicated, may hold values from 0.25 to 1.75
Outputs:
- next_stream: bfloat16 [8192, 2048], P('ep', 'tp')
- next_normed: bfloat16 [8192, 2048], P('ep', 'tp')
The draws below stay inside these ranges and needn't reach their ends.
Inputs may be any that keep to these rules, and one draw needn't show every extreme that they name: `routes`: each row names 6 different experts. Among the 256 rows of one block no expert is named by more than 40 rows, a bound that some block reaches. The live rows of block b are its first live_rows[b] rows; in every draw some block is entirely live.
All inputs are finite; a program needn't handle non-finite values.
Results may differ from the reference program's by a relative error of at most 0.012.
Values may be sent and summed in bfloat16 or wider, within the bound.
A program may use at most 128 MiB of HBM per device.

```python
import math
from functools import partial
import jax
import jax.numpy as jnp
import numpy as np
from jax import lax

D = 2048
ATTN = 2048
FF = 1408
TOP = 6
TOK_DEV = 256
EXPERTS = 64
SHARED_FF = 2816
OWNERS = 32
UNIT_BLOCKS = 4
TOKENS = 8192
CAP = 40


def draw_residual(key, part):
    base_key, column_key, row_key = jax.random.split(jax.random.fold_in(key, 11), 3)
    column_scale = 10.0 ** (jnp.arange(D, dtype=jnp.float32) / D - 0.5) * jax.random.uniform(column_key, (D,), jnp.float32, 0.7, 1.3)
    row_scale = 10.0 ** jax.random.uniform(row_key, (TOKENS, 1), jnp.float32, -0.5, 0.5)
    base = jnp.clip(jax.random.normal(base_key, (TOKENS, D), jnp.float32), -3.0, 3.0)
    return (base * column_scale[None, :] * row_scale).astype(jnp.bfloat16)


def draw_live_rows(key, part):
    count_key, full_key = jax.random.split(jax.random.fold_in(key, 23))
    counts = jax.random.randint(count_key, (OWNERS,), TOK_DEV // 2, TOK_DEV + 1)
    chosen = jax.random.randint(full_key, (), 0, OWNERS)
    return jnp.where(jnp.arange(OWNERS) == chosen, TOK_DEV, counts).astype(jnp.int32)


def level_of(rng, extent, cuts, least, high):
    def one(dim, shards_of):
        steps = jax.random.uniform(jax.random.fold_in(jax.random.fold_in(rng, 6), dim), (shards_of,), jnp.float32, least / len(cuts), high / len(cuts))
        return jnp.repeat(jnp.exp(steps), extent[dim] // shards_of).reshape((-1,) + (1,) * (len(extent) - dim - 1))

    loudness = one(*cuts[0])
    for cut in cuts[1:]:
        loudness = loudness * one(*cut)
    return loudness


def routed_block(key, own, number, rows, number_of, top, reach, skew):
    ranking = jax.random.permutation(key, number_of)
    heavy_load, usual = shares(number_of, rows * top, reach, skew, True), shares(number_of, rows * top, reach, skew, False)
    places = jnp.arange(number_of)

    def named(tallies, rotation):
        used = int((tallies > 0).sum())
        fixed = max(1, used // 4)
        moved = fixed + (places - fixed + rotation * (used - fixed)) % max(1, number_of - fixed)
        return jnp.zeros((number_of,), jnp.int32).at[ranking[jnp.where(places < fixed, places, moved)]].set(jnp.asarray(tallies, jnp.int32))

    tallies = jnp.where(number % 4 == 0, named(heavy_load, number // 4), named(usual, number - number // 4 - 1))
    mixed = jax.random.permutation(jax.random.fold_in(own, 3), number_of)
    source_of, receiver = mixed[0:number_of // 2 * 2:2], mixed[1:number_of // 2 * 2:2]
    margin = jnp.minimum(tallies[source_of] - 1, reach - tallies[receiver]) // 2
    margin = jnp.where((source_of == ranking[0]) | (receiver == ranking[0]) | (tallies[receiver] == 0), 0, jnp.maximum(margin, 0))
    moved = jax.random.randint(jax.random.fold_in(own, 4), (number_of // 2,), 0, 1 << 20) % (margin + 1)
    tallies = tallies.at[source_of].add(-moved).at[receiver].add(moved)
    members = jnp.searchsorted(jnp.cumsum(tallies), jnp.arange(rows * top), side="right").astype(jnp.int32)
    table = members.reshape(top, rows).T
    table = table[jax.random.permutation(jax.random.fold_in(own, 1), rows)]
    rotation = jax.random.randint(jax.random.fold_in(own, 2), (rows, 1), 0, top)
    return jnp.take_along_axis(table, (jnp.arange(top)[None, :] + rotation) % top, axis=1)


def shares(number_of, total, reach, lean, full):
    loads = [(1 << 20) // math.isqrt(rank ** lean) + 1 for rank in range(1, number_of + 1)]
    largest = reach if full else min(reach, max(-(-total // number_of), total * loads[0] // sum(loads)))
    least = 1 if total - largest >= number_of - 1 else 0
    holding, rest = [largest] + [least] * (number_of - 1), total - largest - least * (number_of - 1)
    while rest > 0:
        candidates = [i for i in range(1, number_of) if holding[i] < largest] or [i for i in range(1, number_of) if holding[i] < reach]
        whole, left = sum([loads[i] for i in candidates]), rest
        for i in candidates:
            extra = min(reach - holding[i], max(1, left * loads[i] // whole), rest)
            holding[i] = holding[i] + extra
            rest = rest - extra
    return np.array(holding)


def noise(stream_key, shape, spread, bound, pieces=(), held_as=jnp.bfloat16):
    values = jax.random.normal(stream_key, shape, jnp.float32) * spread
    if len(pieces) > 0:
        values = level_of(stream_key, shape, pieces, -0.22, 0.18) * values
    return jnp.clip(values, min=-bound, max=bound).astype(held_as)


def setup_inputs(seed: int = 0) -> dict:
    key_list = jax.random.split(jax.random.key(seed), 13)
    attn_out = noise(key_list[0], (TOKENS, ATTN), 1.0, 6.0, ((0, 32), (1, 8)))
    out_proj = noise(key_list[1], (ATTN, D), ATTN ** -0.5, 0.125, ((0, 8),))
    residual = draw_residual(jax.random.fold_in(key_list[12], 71), 0)
    norm_gain = jnp.clip(1.0 + 0.15 * jax.random.normal(key_list[3], (D,), jnp.float32), 0.25, 1.75)
    router = noise(key_list[4], (D, EXPERTS), D ** -0.5, 0.125)
    expert_gate_up = noise(key_list[5], (EXPERTS * UNIT_BLOCKS, 2, FF // UNIT_BLOCKS, D), D ** -0.5, 0.125, ((0, 256),))
    expert_down = noise(key_list[6], (EXPERTS * UNIT_BLOCKS, FF // UNIT_BLOCKS, D), FF ** -0.5, 0.15625, ((0, 256),))
    shared_gate_up = noise(key_list[7], (2, SHARED_FF, D), D ** -0.5, 0.125, ((1, 8),))
    shared_down = noise(key_list[8], (SHARED_FF, D), SHARED_FF ** -0.5, 0.109375, ((0, 8),))
    routes_keys = jax.random.split(jax.random.fold_in(key_list[9], 1), TOKENS // TOK_DEV)
    routes_turns = jax.random.permutation(jax.random.fold_in(key_list[9], 3), TOKENS // TOK_DEV)
    routes = jax.vmap(lambda own, number: routed_block(jax.random.fold_in(key_list[9], 2), own, number, TOK_DEV, EXPERTS, TOP, CAP, 2))(routes_keys, routes_turns).reshape((TOKENS, TOP))
    live_rows = draw_live_rows(jax.random.fold_in(key_list[12], 71), 0)
    next_gain = jnp.clip(1.0 + 0.15 * jax.random.normal(key_list[11], (D,), jnp.float32), 0.25, 1.75)
    return {"attn_out": attn_out, "out_proj": out_proj, "residual": residual, "norm_gain": norm_gain, "router": router, "expert_gate_up": expert_gate_up, "expert_down": expert_down, "shared_gate_up": shared_gate_up, "shared_down": shared_down, "routes": routes, "live_rows": live_rows, "next_gain": next_gain}


norm_epsilon = 1e-06
routed_scale = 2.446

def root_norm(values, gain):
    return values * lax.rsqrt(lax.optimization_barrier(jnp.mean(values * values, axis=-1, keepdims=True)) + norm_epsilon) * gain

def slot_table(route_block, live_count, experts, capacity):
    fanout = route_block.shape[1]
    flat_ids = route_block.reshape(-1)
    entry_index = jnp.arange(flat_ids.shape[0], dtype=jnp.int32)
    living = entry_index // fanout < live_count
    one_hot = ((flat_ids[:, None] == jnp.arange(experts, dtype=jnp.int32)[None, :]) & living[:, None]).astype(jnp.int32)
    earlier = jnp.cumsum(one_hot, axis=0, dtype=jnp.int32) - one_hot
    position = lax.optimization_barrier(jnp.sum(earlier * one_hot, axis=1, dtype=jnp.int32))
    slot_index = jnp.where(living, flat_ids * capacity + position, experts * capacity).astype(jnp.int32)
    slot_owner = jnp.full((experts * capacity,), -1, jnp.int32).at[slot_index].set(entry_index, mode='drop')
    return (slot_index, living, slot_owner)

def gate_weights(normed, router, route_block):
    logits = jnp.dot(normed, router, preferred_element_type=jnp.float32)
    chosen = jnp.take_along_axis(logits, route_block, axis=1)
    scores = jax.nn.sigmoid(chosen)
    return scores / lax.optimization_barrier(jnp.sum(scores, axis=1, keepdims=True)) * routed_scale

def pick_rows(table, indices):
    return table[indices]

def reference(attn_out, out_proj, residual, norm_gain, router, expert_gate_up, expert_down, shared_gate_up, shared_down, routes, live_rows, next_gain):
    stream = (jnp.dot(attn_out, out_proj, preferred_element_type=jnp.float32) + residual.astype(jnp.float32)).astype(jnp.bfloat16)
    normed = root_norm(stream.astype(jnp.float32), norm_gain).astype(jnp.bfloat16)
    blocks = live_rows.shape[0]
    per_block = stream.shape[0] // blocks
    experts = router.shape[1]
    fanout = routes.shape[1]
    width = stream.shape[1]
    route_blocks = routes.reshape(blocks, per_block, fanout)
    normed_blocks = normed.reshape(blocks, per_block, width)
    slot_index, living, slot_owner = jax.vmap(partial(slot_table, experts=experts, capacity=CAP))(route_blocks, live_rows)
    filled = slot_owner >= 0
    source_row = jnp.where(filled, slot_owner // fanout, 0)
    dispatched = jax.vmap(pick_rows)(normed_blocks, source_row)
    dispatched = jnp.where(filled[:, :, None], dispatched, jnp.zeros((), dispatched.dtype))
    expert_rows = jnp.swapaxes(dispatched.reshape(blocks, experts, CAP, width), 0, 1).reshape(experts, blocks * CAP, width)
    unit_width = FF // UNIT_BLOCKS
    gate_up_all = expert_gate_up.reshape(experts, UNIT_BLOCKS, 2, unit_width, width)
    down_all = expert_down.reshape(experts, UNIT_BLOCKS, unit_width, width)

    def run_expert(operands):
        row_block, gate_up, down_weight = operands
        running = jnp.zeros((row_block.shape[0], width), jnp.float32)
        for unit_index in range(UNIT_BLOCKS):
            gate_proj = jnp.dot(row_block, gate_up[unit_index, 0].T, preferred_element_type=jnp.float32)
            up_proj = jnp.dot(row_block, gate_up[unit_index, 1].T, preferred_element_type=jnp.float32)
            hidden = (jax.nn.silu(gate_proj) * up_proj).astype(jnp.bfloat16)
            piece = jnp.dot(hidden, down_weight[unit_index], preferred_element_type=jnp.float32).astype(jnp.bfloat16)
            piece = lax.optimization_barrier(piece)
            running = running + piece.astype(jnp.float32)
        return running
    produced = lax.map(run_expert, (expert_rows, gate_up_all, down_all))
    returned = jnp.swapaxes(produced.reshape(experts, blocks, CAP, width), 0, 1).reshape(blocks, experts * CAP, width)
    picked = jax.vmap(pick_rows)(returned, jnp.minimum(slot_index, experts * CAP - 1))
    picked = picked.reshape(blocks, per_block, fanout, width)
    weights = gate_weights(normed, router, routes).reshape(blocks, per_block, fanout)
    weights = weights * living.reshape(blocks, per_block, fanout).astype(jnp.float32)
    routed = lax.optimization_barrier(jnp.sum(picked * weights[:, :, :, None], axis=2)).reshape(blocks * per_block, width)
    shared_gate = jnp.dot(normed, shared_gate_up[0].T, preferred_element_type=jnp.float32)
    shared_up = jnp.dot(normed, shared_gate_up[1].T, preferred_element_type=jnp.float32)
    shared_hidden = (jax.nn.silu(shared_gate) * shared_up).astype(jnp.bfloat16)
    shared_out = jnp.dot(shared_hidden, shared_down, preferred_element_type=jnp.float32)
    next_stream = (stream.astype(jnp.float32) + shared_out + routed).astype(jnp.bfloat16)
    next_normed = root_norm(next_stream.astype(jnp.float32), next_gain).astype(jnp.bfloat16)
    return (next_stream, next_normed)
```

```python
import jax
import jax.numpy as jnp
from jax import lax
from jax.experimental import pallas as pl
from jax.experimental.pallas import tpu as pltpu
from jax.sharding import PartitionSpec as P

NX, NZ, NY = 4, 8, 4
CAP = 40
PAIRS = {0: (0, 4), 1: (1, 7), 2: (2, 6), 3: (3, 5)}
EPS = 1e-06
SCALE = 2.446
F32 = jnp.float32
BF16 = jnp.bfloat16
MESH = pl.DeviceIdType.MESH


def dot_nn(a, b):
    return lax.dot_general(a, b, (((1,), (0,)), ((), ())), preferred_element_type=F32)


def dot_nt(a, b):
    return lax.dot_general(a, b, (((1,), (1,)), ((), ())), preferred_element_type=F32)


def dot_tn(a, b):
    return lax.dot_general(a, b, (((0,), (0,)), ((), ())), preferred_element_type=F32)


def kernel(
    live_ref, attn_h, proj_h, resid_h, gain_h, router_h, gu_h, dn_h, sgu_h, sdn_h, routes_h, ngain_h,
    out_s, out_n,
    attn, proj, resid, gain, router, gu, dn, sgu, sdn, routes, ngain,
    d2d_s, d2d_r, ys, yr, st, own_acc, ss_s, ss_r,
    code, cz, gt, gz, msel,
    nb, nsib, pmat, wmat, xs, rows, rsib,
    gbuf, hbuf, tsnd, trcv, town, rt,
    sh_own, sh_s, sh_r,
    pb, ysnd, yrcv, rs_s, rs_r, fb_s, fb_r, q_s, q_r,
    load_sem, local_sem, send_sem, recv_sem,
):
    ep = lax.axis_index("ep")
    tp = lax.axis_index("tp")
    x, z = ep // NZ, lax.rem(ep, NZ)
    y, c = tp // 2, lax.rem(tp, 2)
    grp = y // 2
    sc = 1 - c
    T = attn.shape[0]
    W = attn.shape[1]
    FFP = gu.shape[0] // 2
    FF = gu_h.shape[2]

    def at_y(k):
        return lax.rem(y + k, NY)

    def at_z(k):
        return lax.rem(z + k, NZ)

    def at_x(k):
        return lax.rem(x + k, NX)

    def dev(xx=None, zz=None, yy=None, cc=None):
        xx = x if xx is None else xx
        zz = z if zz is None else zz
        yy = y if yy is None else yy
        cc = c if cc is None else cc
        return (xx * NZ + zz, yy * 2 + cc)

    sibling = dev(cc=sc)

    def col(rel, core):
        return pl.multiple_of((at_y(rel) * 2 + core) * W, W)

    copies = []

    def send(src, dst, to):
        i = len(copies)
        cp = pltpu.make_async_remote_copy(
            src_ref=src, dst_ref=dst, send_sem=send_sem.at[i], recv_sem=recv_sem.at[i],
            device_id=to, device_id_type=MESH,
        )
        cp.start()
        copies.append(cp)
        return cp

    loads = []

    def load(src, dst):
        i = len(loads)
        cp = pltpu.make_async_copy(src, dst, load_sem.at[i])
        cp.start()
        loads.append(cp)
        return cp

    locals_ = []

    def local(src, dst):
        i = len(locals_)
        cp = pltpu.make_async_copy(src, dst, local_sem.at[i])
        cp.start()
        locals_.append(cp)
        return cp

    l_attn = load(attn_h, attn)
    l_proj = load(proj_h, proj)
    l_routes = load(routes_h, routes)
    l_resid = load(resid_h.at[:, pl.ds(col(0, c), W)], resid)
    l_gain = load(gain_h, gain)
    l_ngain = load(ngain_h, ngain)
    l_router = load(router_h, router)
    l_sg = load(sgu_h.at[0], sgu.at[pl.ds(0, FF)])
    l_su = load(sgu_h.at[1], sgu.at[pl.ds(FFP, FF)])
    l_sd = load(sdn_h, sdn.at[pl.ds(0, FF)])
    l_g = load(gu_h.at[0, 0], gu.at[pl.ds(0, FF)])
    l_u = load(gu_h.at[0, 1], gu.at[pl.ds(FFP, FF)])
    l_d = load(dn_h.at[0], dn.at[pl.ds(0, FF)])

    peers = [sibling]
    peers += [dev(yy=at_y(k)) for k in (1, 2, 3)]
    peers += [dev(yy=at_y(k), cc=sc) for k in (1, 2, 3)]
    peers += [dev(xx=at_x(k)) for k in (1, 2, 3)]
    peers += [dev(zz=at_z(k)) for k in range(1, NZ)]
    barrier = pltpu.get_barrier_semaphore()
    for peer in peers:
        pl.semaphore_signal(barrier, inc=1, device_id=peer, device_id_type=MESH)

    zpad = jnp.zeros((FFP - FF, gu.shape[1]), BF16)
    for ref in (gu, sgu):
        ref[FF:FFP, :] = zpad
        ref[FFP + FF : 2 * FFP, :] = zpad
    for ref in (dn, sdn):
        ref[FF:FFP, :] = zpad

    l_attn.wait()
    l_proj.wait()
    for rel in (2, 1, 3, 0):
        d2d_s[rel] = dot_nn(attn[...], proj[:, pl.ds(col(rel, sc), W)]).astype(BF16)
    pl.semaphore_wait(barrier, len(peers))
    c_d2d = {rel: send(d2d_s.at[rel], d2d_r.at[rel], sibling) for rel in (2, 1, 3, 0)}
    c_yr = {}
    for rel in (2, 1, 3):
        part = dot_nn(attn[...], proj[:, pl.ds(col(rel, c), W)])
        c_d2d[rel].wait_recv()
        ys[rel - 1] = (part + d2d_r[rel].astype(F32)).astype(BF16)
        c_yr[rel] = send(ys.at[rel - 1], yr.at[rel - 1], dev(yy=at_y(rel)))
    part = dot_nn(attn[...], proj[:, pl.ds(col(0, c), W)])
    c_d2d[0].wait_recv()
    l_resid.wait()
    own_acc[...] = part + d2d_r[0].astype(F32) + resid[...].astype(F32)

    l_routes.wait()
    experts = NX * NZ * 2
    lane_e = lax.broadcasted_iota(jnp.int32, (T, experts), 1)
    chosen = lane_e == routes[:, 0:1]
    for k in range(1, routes.shape[1]):
        chosen = chosen | (lane_e == routes[:, k : k + 1])
    token = lax.broadcasted_iota(jnp.int32, (T, experts), 0)
    alive = token < live_ref[0]
    msel[...] = jnp.where(chosen, 1.0, 0.0)
    active = jnp.where(chosen & alive, 1.0, 0.0).astype(BF16)
    r = lax.broadcasted_iota(jnp.int32, (experts, experts), 0)
    e = lax.broadcasted_iota(jnp.int32, (experts, experts), 1)
    wanted = 2 * ((r & 3) * NZ + (r >> 3)) + ((r >> 2) & 1)
    perm = jnp.where(e == wanted, 1.0, 0.0).astype(BF16)
    act_t = dot_nt(perm, active)
    before = jnp.where(
        lax.broadcasted_iota(jnp.int32, (T, T), 0) < lax.broadcasted_iota(jnp.int32, (T, T), 1), 1.0, 0.0
    ).astype(BF16)
    position = dot_nn(act_t.astype(BF16), before)
    code[...] = jnp.where(act_t > 0.5, position, -1.0)
    c_code = {}
    for k in range(1, NZ):
        c_code[k] = send(
            code.at[pl.ds(pl.multiple_of(at_z(k) * 8, 8), 8)], cz.at[k], dev(zz=at_z(k))
        )
    cz[0] = code[pl.ds(pl.multiple_of(z * 8, 8), 8), :]

    for rel in (1, 3, 2):
        c_yr[rel].wait_recv()
    total = own_acc[...]
    for k in range(3):
        total = total + yr[k].astype(F32)
    st[0] = total.astype(BF16)
    c_st = {rel: send(st.at[0], st.at[rel], dev(yy=at_y(NY - rel))) for rel in (2, 1, 3)}
    for rel in (1, 3, 2):
        c_st[rel].wait_recv()

    sq = None
    for rel in range(4):
        v = st[rel].astype(F32)
        v = v * v
        for k in range(W // 128):
            piece = v[:, k * 128 : (k + 1) * 128]
            sq = piece if sq is None else sq + piece
    ss_s[...] = sq
    c_ss = send(ss_s, ss_r, sibling)
    l_gain.wait()
    c_ss.wait_recv()
    mean = jnp.sum(ss_s[...] + ss_r[...], axis=1, keepdims=True) / (8 * W)
    inv = lax.rsqrt(mean + EPS)

    def gain_row(ref, rel):
        return ref[pl.ds(at_y(rel) * 2 + c, 1), :]

    z_right, z_left = dev(zz=at_z(1)), dev(zz=at_z(NZ - 1))
    y_up, y_down = dev(yy=at_y(1)), dev(yy=at_y(NY - 1))
    ring = {}
    yfw = {}
    for rel in range(4):
        nb[0, rel] = (st[rel].astype(F32) * inv * gain_row(gain, rel)).astype(BF16)
        if rel < 2:
            ring["R", 0, rel] = send(nb.at[0, rel], nb.at[1, rel], z_right)
            ring["L", 0, rel] = send(nb.at[0, rel], nb.at[NZ - 1, rel], z_left)
    c_sib = send(nb.at[0], nsib, sibling)

    def ring_step(s):
        for way, got, nxt in (("R", s + 1, s + 2), ("L", NZ - 1 - s, NZ - 2 - s)):
            for ch in (0, 1):
                if s == 3 and ch != (0 if way == "R" else 1):
                    continue
                ring[way, s, ch].wait_recv()
                if s < 2 or (s == 2 and ch == (0 if way == "R" else 1)):
                    ring[way, s + 1, ch] = send(
                        nb.at[got, ch], nb.at[nxt, ch], z_right if way == "R" else z_left
                    )
                if ch == 0:
                    yfw[got, 3] = send(nb.at[got, 0], nb.at[got, 3], y_up)
                else:
                    yfw[got, 2] = send(nb.at[got, 1], nb.at[got, 2], y_down)

    slot_id = lax.broadcasted_iota(jnp.int32, (CAP, T), 0).astype(F32)
    none = jnp.zeros((CAP, T), F32)

    def build_slots(p):
        a, b = PAIRS[p]
        for k in (a, b):
            if k > 0:
                c_code[k].wait_recv()
        for xp in range(NX):
            ca = cz[a, pl.ds(grp * 4 + xp, 1), :]
            cb = cz[b, pl.ds(grp * 4 + xp, 1), :]
            pa = jnp.where(slot_id == ca, 1.0, 0.0)
            pb_ = jnp.where(slot_id == cb, 1.0, 0.0)
            block = jnp.concatenate(
                [jnp.concatenate([pa, none], axis=1), jnp.concatenate([none, pb_], axis=1)], axis=0
            )
            pmat[p, xp * 2 * CAP : (xp + 1) * 2 * CAP, :] = block.astype(BF16)

    c_x = {}
    l_x = {}
    R = 2 * CAP

    def slots(p):
        a, b = PAIRS[p]
        for rel in range(4):
            picked = dot_nn(pmat[p, :, 0:T], nb[a, rel]) + dot_nn(pmat[p, :, T : 2 * T], nb[b, rel])
            xs[p, :, rel * W : (rel + 1) * W] = picked.astype(BF16)
        here = pl.ds(pl.multiple_of(x * R, R), R)
        for k in (2, 1, 3):
            there = pl.ds(pl.multiple_of(at_x(k) * R, R), R)
            c_x[p, k] = send(xs.at[p, there], rows.at[p, here], dev(xx=at_x(k)))
        l_x[p] = local(xs.at[p, here], rows.at[p, here])

    c_fw = {}

    def forward(p):
        l_x[p].wait()
        for k in (1, 3, 2):
            c_x[p, k].wait_recv()
        c_fw[p] = send(rows.at[p], rsib.at[p], sibling)

    def swiglu(m, own, sib, weights):
        def up(n, carry):
            units = pl.ds(pl.multiple_of(n * 256, 256), 256)
            acc = None
            for rel in range(4):
                t = dot_nt(own(rel), weights[units, pl.ds(col(rel, c), W)])
                acc = t if acc is None else acc + t
            for rel in range(4):
                acc = acc + dot_nt(sib(rel), weights[units, pl.ds(col(rel, sc), W)])
            gbuf[0:m, units] = acc
            return carry

        lax.fori_loop(0, 2 * FFP // 256, up, 0)

        def act(i, carry):
            part = pl.ds(pl.multiple_of(i * (m // 4), 16), m // 4)
            gate = gbuf[part, 0:FFP]
            hbuf[part, :] = (gate / (1.0 + jnp.exp(-gate)) * gbuf[part, FFP : 2 * FFP]).astype(BF16)
            return carry

        lax.fori_loop(0, 4, act, 0)

    c_t = {}

    def expert(p):
        c_fw[p].wait_recv()
        swiglu(
            NX * R,
            lambda rel: rows[p, :, rel * W : (rel + 1) * W],
            lambda rel: rsib[p, :, rel * W : (rel + 1) * W],
            gu,
        )
        for rel in range(4):
            t = dot_nn(hbuf[...], dn[:, pl.ds(col(rel, sc), W)])
            tsnd[p, :, rel * W : (rel + 1) * W] = t.astype(BF16)
        c_t[p] = send(tsnd.at[p], trcv.at[p], sibling)
        for rel in range(4):
            t = dot_nn(hbuf[...], dn[:, pl.ds(col(rel, c), W)])
            town[p, :, rel * W : (rel + 1) * W] = t.astype(BF16)

    c_ret = {}
    l_ret = {}

    def give_back(p):
        c_t[p].wait_recv()
        town[p] = (town[p].astype(F32) + trcv[p].astype(F32)).astype(BF16)
        here = pl.ds(pl.multiple_of(x * R, R), R)
        for k in (2, 1, 3):
            there = pl.ds(pl.multiple_of(at_x(k) * R, R), R)
            c_ret[p, k] = send(town.at[p, there], rt.at[p, here], dev(xx=at_x(k)))
        l_ret[p] = local(town.at[p, here], rt.at[p, here])

    c_y = {}

    def combine(p):
        a, b = PAIRS[p]
        for k in (a, b):
            if k > 0:
                c_gate[k].wait_recv()
        for xp in range(NX):
            ga = gz[a, pl.ds(grp * 4 + xp, 1), :]
            gb = gz[b, pl.ds(grp * 4 + xp, 1), :]
            g2 = jnp.concatenate([ga, gb], axis=1)
            part = slice(xp * R, (xp + 1) * R)
            wmat[part, :] = (pmat[p, part, :].astype(F32) * g2).astype(BF16)
        l_ret[p].wait()
        for k in (1, 3, 2):
            c_ret[p, k].wait_recv()
        for rel in (2, 3, 0, 1):
            for half, k in ((0, a), (1, b)):
                got = dot_tn(wmat[:, half * T : (half + 1) * T], rt[p, :, rel * W : (rel + 1) * W])
                if k == 0:
                    got = got + sh_own[rel].astype(F32) + sh_r[rel].astype(F32)
                if rel < 2:
                    pb[k, rel] = got
                elif rel == 2:
                    ysnd[k, 0] = got.astype(BF16)
                    c_y[k, 1] = send(ysnd.at[k, 0], yrcv.at[k, 1], y_up)
                else:
                    ysnd[k, 1] = got.astype(BF16)
                    c_y[k, 0] = send(ysnd.at[k, 1], yrcv.at[k, 0], y_down)

    for p in (1, 2, 3, 0):
        build_slots(p)
    l_router.wait()
    c_sib.wait_recv()
    logits = None
    for rel in range(4):
        t = dot_nn(nb[0, rel], router[pl.ds(col(rel, c), W), :])
        t = t + dot_nn(nsib[rel], router[pl.ds(col(rel, sc), W), :])
        logits = t if logits is None else logits + t
    scores = msel[...] / (1.0 + jnp.exp(-logits))
    gates = scores / jnp.sum(scores, axis=1, keepdims=True) * SCALE
    gates = jnp.where(alive, gates, 0.0).astype(BF16)
    gt[...] = dot_nt(perm, gates)
    c_gate = {}
    for k in range(1, NZ):
        c_gate[k] = send(gt.at[pl.ds(pl.multiple_of(at_z(k) * 8, 8), 8)], gz.at[k], dev(zz=at_z(k)))
    gz[0] = gt[pl.ds(pl.multiple_of(z * 8, 8), 8), :]

    def wait_y(p):
        for k in PAIRS[p]:
            if k > 0:
                yfw[k, 2].wait_recv()
                yfw[k, 3].wait_recv()

    ring_step(0)
    l_sg.wait()
    l_su.wait()
    l_sd.wait()
    swiglu(T, lambda rel: nb[0, rel], lambda rel: nsib[rel], sgu)
    for rel in range(4):
        sh_s[rel] = dot_nn(hbuf[0:T, :], sdn[:, pl.ds(col(rel, sc), W)]).astype(BF16)
    c_sh = send(sh_s, sh_r, sibling)
    for rel in range(4):
        sh_own[rel] = dot_nn(hbuf[0:T, :], sdn[:, pl.ds(col(rel, c), W)])
    wait_y(1)
    slots(1)
    ring_step(1)
    wait_y(2)
    slots(2)
    forward(1)
    ring_step(2)
    wait_y(3)
    slots(3)
    l_g.wait()
    l_u.wait()
    l_d.wait()
    expert(1)
    ring_step(3)
    wait_y(0)
    slots(0)
    give_back(1)
    forward(2)
    expert(2)
    give_back(2)
    forward(3)
    expert(3)
    give_back(3)
    combine(1)
    forward(0)
    expert(0)
    give_back(0)
    combine(2)
    combine(3)
    c_sh.wait_recv()
    combine(0)

    back = {}

    def value(k, ch):
        c_y[k, ch].wait_recv()
        return pb[k, ch] + yrcv[k, ch].astype(F32)

    for s in range(4):
        for wi, way, k, to in ((0, "L", 4 - s, z_left), (1, "R", 4 + s, z_right)):
            for ch in (0, 1):
                if s == 0 and ch != wi:
                    continue
                if s == 0 and wi == 1:
                    v = value(4, 1)
                else:
                    v = value(k, ch)
                if (way, s - 1, ch) in back:
                    back[way, s - 1, ch].wait_recv()
                    v = v + rs_r[wi, s - 1, ch].astype(F32)
                rs_s[wi, s, ch] = v.astype(BF16)
                back[way, s, ch] = send(rs_s.at[wi, s, ch], rs_r.at[wi, s, ch], to)

    def finish(ch):
        v = value(0, ch)
        for wi, way in ((0, "L"), (1, "R")):
            back[way, 3, ch].wait_recv()
            v = v + rs_r[wi, 3, ch].astype(F32)
        return v

    fb_s[...] = finish(1).astype(BF16)
    c_fb = send(fb_s, fb_r, y_up)
    mine = finish(0) + st[0].astype(F32)
    c_fb.wait_recv()
    nxt = (mine + fb_r[...].astype(F32)).astype(BF16)
    out_s[...] = nxt
    wide = nxt.astype(F32)
    ones = jnp.ones((8, W), F32)
    q_s[...] = lax.dot_general(
        ones, wide * wide, (((1,), (1,)), ((), ())), precision=lax.Precision.HIGHEST, preferred_element_type=F32
    )
    c_q = [send(q_s, q_r.at[0], sibling)]
    for k in (1, 2, 3):
        c_q.append(send(q_s, q_r.at[k], dev(yy=at_y(k))))
        c_q.append(send(q_s, q_r.at[3 + k], dev(yy=at_y(k), cc=sc)))
    l_ngain.wait()
    for cp in c_q:
        cp.wait_recv()
    tot = q_s[...]
    for k in range(7):
        tot = tot + q_r[k]
    inv_t = lax.rsqrt(tot / (8 * W) + EPS)
    inv2 = jnp.transpose(inv_t)[:, 0:1]
    out_n[...] = (wide * inv2 * gain_row(ngain, 0)).astype(BF16)
    for cp in copies:
        cp.wait_send()


N_SEND = 160


def on_device(
    attn_out, out_proj, residual, norm_gain, router, expert_gate_up, expert_down,
    shared_gate_up, shared_down, routes, live_rows, next_gain,
):
    T, W = attn_out.shape
    D = out_proj.shape[1]
    FF = expert_down.shape[1]
    FFP = -(-FF // 128) * 128
    H = D // 2
    R4 = NX * 2 * CAP
    fanout = routes.shape[1]
    vm = pltpu.VMEM
    scratch = [
        vm((T, W), BF16), vm((W, D), BF16), vm((T, W), BF16), vm((8, W), F32), vm((D, 64), BF16),
        vm((2 * FFP, D), BF16), vm((FFP, D), BF16), vm((2 * FFP, D), BF16), vm((FFP, D), BF16),
        vm((T, fanout), jnp.int32), vm((8, W), F32),
        vm((4, T, W), BF16), vm((4, T, W), BF16), vm((3, T, W), BF16), vm((3, T, W), BF16),
        vm((4, T, W), BF16), vm((T, W), F32), vm((T, 128), F32), vm((T, 128), F32),
        vm((64, T), F32), vm((NZ, 8, T), F32), vm((64, T), F32), vm((NZ, 8, T), F32), vm((T, 64), F32),
        vm((NZ, 4, T, W), BF16), vm((4, T, W), BF16), vm((4, R4, 2 * T), BF16), vm((R4, 2 * T), BF16),
        vm((4, R4, H), BF16), vm((4, R4, H), BF16), vm((4, R4, H), BF16),
        vm((R4, 2 * FFP), F32), vm((R4, FFP), BF16),
        vm((4, R4, H), BF16), vm((4, R4, H), BF16), vm((4, R4, H), BF16), vm((4, R4, H), BF16),
        vm((4, T, W), F32), vm((4, T, W), BF16), vm((4, T, W), BF16),
        vm((NZ, 2, T, W), F32), vm((NZ, 2, T, W), BF16), vm((NZ, 2, T, W), BF16),
        vm((2, 4, 2, T, W), BF16), vm((2, 4, 2, T, W), BF16),
        vm((T, W), BF16), vm((T, W), BF16), vm((8, T), F32), vm((7, 8, T), F32),
        pltpu.SemaphoreType.DMA((13,)), pltpu.SemaphoreType.DMA((8,)),
        pltpu.SemaphoreType.DMA((N_SEND,)), pltpu.SemaphoreType.DMA((N_SEND,)),
    ]
    hbm = pl.BlockSpec(memory_space=pl.ANY)
    return pl.pallas_call(
        kernel,
        out_shape=(jax.ShapeDtypeStruct((T, W), BF16), jax.ShapeDtypeStruct((T, W), BF16)),
        in_specs=[pl.BlockSpec(memory_space=pltpu.SMEM)] + [hbm] * 11,
        out_specs=(pl.BlockSpec(memory_space=pltpu.VMEM), pl.BlockSpec(memory_space=pltpu.VMEM)),
        scratch_shapes=scratch,
        compiler_params=pltpu.CompilerParams(
            collective_id=0, has_side_effects=True, vmem_limit_bytes=67043328
        ),
    )(
        live_rows, attn_out, out_proj, residual, norm_gain.reshape(8, W), router, expert_gate_up,
        expert_down, shared_gate_up, shared_down, routes, next_gain.reshape(8, W),
    )


def solution(mesh):
    in_specs = (
        P("ep", "tp"),
        P("tp", None),
        P("ep", None),
        P(),
        P(),
        P(("ep", "tp"), None, None, None),
        P(("ep", "tp"), None, None),
        P(None, "tp", None),
        P("tp", None),
        P("ep", None),
        P("ep"),
        P(),
    )
    out_specs = (P("ep", "tp"), P("ep", "tp"))
    return jax.shard_map(
        on_device, mesh=mesh, in_specs=in_specs, out_specs=out_specs, check_vma=False
    )
```

```python
import jax
import jax.numpy as jnp
from jax import lax
from jax.experimental import pallas as pl
from jax.experimental.pallas import tpu as pltpu
from jax.sharding import PartitionSpec as P

NX, NZ, NY = 4, 8, 4
CAP = 40
CAP_PAD = 48
BLOCKS = {0: (0,), 1: (1, 7), 2: (2, 6), 3: (3, 5), 4: (4,)}
EPS = 1e-06
SCALE = 2.446
F32 = jnp.float32
BF16 = jnp.bfloat16
MESH = pl.DeviceIdType.MESH


def dot_nn(a, b):
    return lax.dot_general(a, b, (((1,), (0,)), ((), ())), preferred_element_type=F32)


def dot_nt(a, b):
    return lax.dot_general(a, b, (((1,), (1,)), ((), ())), preferred_element_type=F32)


def dot_tn(a, b):
    return lax.dot_general(a, b, (((0,), (0,)), ((), ())), preferred_element_type=F32)


def kernel(
    live_ref, attn_h, proj_h, resid_h, gain_h, router_h, gu_h, dn_h, sgu_h, sdn_h, routes_h, ngain_h,
    out_s, out_n,
    attn, proj, resid, gain1, gain, router, gu, dn, sgu, sdn, routes, ngain1, ngain,
    d2d_s, d2d_r, ys, yr, st, own_acc, ss_s, ss_r,
    code, cz, gt, gz,
    nb, nsib, pmat2, pmat1, wmat2, wmat1, xs2, xs1, rows2, rows1, rsib2, rsib1,
    gbuf, hbuf, tsnd2, tsnd1, trcv2, trcv1, town2, town1, rt2, rt1,
    sh_own, sh_s, sh_r,
    pb, ysnd, yrcv, rs_s, rs_r, fb_s, fb_r, q_s, q_r,
    load_sem, local_sem, send_sem, recv_sem,
):
    ep = lax.axis_index("ep")
    tp = lax.axis_index("tp")
    x, z = ep // NZ, lax.rem(ep, NZ)
    y, c = tp // 2, lax.rem(tp, 2)
    grp = y // 2
    sc = 1 - c
    T = attn.shape[0]
    W = attn.shape[1]
    FFP = gu.shape[0] // 2
    FF = gu_h.shape[2]

    def chunk(double, single, p):
        return double.at[p - 1] if 1 <= p <= 3 else single.at[p // 4]

    def per_owner(p):
        return 2 * CAP if 1 <= p <= 3 else CAP_PAD

    def at_y(k):
        return lax.rem(y + k, NY)

    def at_z(k):
        return lax.rem(z + k, NZ)

    def at_x(k):
        return lax.rem(x + k, NX)

    def dev(xx=None, zz=None, yy=None, cc=None):
        xx = x if xx is None else xx
        zz = z if zz is None else zz
        yy = y if yy is None else yy
        cc = c if cc is None else cc
        return (xx * NZ + zz, yy * 2 + cc)

    sibling = dev(cc=sc)

    def col(rel, core):
        return pl.multiple_of((at_y(rel) * 2 + core) * W, W)

    copies = []

    def send(src, dst, to):
        i = len(copies)
        cp = pltpu.make_async_remote_copy(
            src_ref=src, dst_ref=dst, send_sem=send_sem.at[i], recv_sem=recv_sem.at[i],
            device_id=to, device_id_type=MESH,
        )
        cp.start()
        copies.append(cp)
        return cp

    loads = []

    def load(src, dst):
        i = len(loads)
        cp = pltpu.make_async_copy(src, dst, load_sem.at[i])
        cp.start()
        loads.append(cp)
        return cp

    locals_ = []

    def local(src, dst):
        i = len(locals_)
        cp = pltpu.make_async_copy(src, dst, local_sem.at[i])
        cp.start()
        locals_.append(cp)
        return cp

    l_attn = load(attn_h, attn)
    l_proj = load(proj_h, proj)
    l_routes = load(routes_h, routes)
    l_resid = load(resid_h.at[:, pl.ds(col(0, c), W)], resid)
    l_gain = load(gain_h, gain1)
    l_ngain = load(ngain_h, ngain1)
    l_router = load(router_h, router)
    l_sg = load(sgu_h.at[0], sgu.at[pl.ds(0, FF)])
    l_su = load(sgu_h.at[1], sgu.at[pl.ds(FFP, FF)])
    l_sd = load(sdn_h, sdn.at[pl.ds(0, FF)])
    l_g = load(gu_h.at[0, 0], gu.at[pl.ds(0, FF)])
    l_u = load(gu_h.at[0, 1], gu.at[pl.ds(FFP, FF)])
    l_d = load(dn_h.at[0], dn.at[pl.ds(0, FF)])

    peers = [sibling]
    peers += [dev(yy=at_y(k)) for k in (1, 2, 3)]
    peers += [dev(yy=at_y(k), cc=sc) for k in (1, 2, 3)]
    peers += [dev(xx=at_x(k)) for k in (1, 2, 3)]
    peers += [dev(zz=at_z(k)) for k in range(1, NZ)]
    barrier = pltpu.get_barrier_semaphore()
    for peer in peers:
        pl.semaphore_signal(barrier, inc=1, device_id=peer, device_id_type=MESH)

    zpad = jnp.zeros((FFP - FF, gu.shape[1]), BF16)
    for ref in (gu, sgu):
        ref[FF:FFP, :] = zpad
        ref[FFP + FF : 2 * FFP, :] = zpad
    for ref in (dn, sdn):
        ref[FF:FFP, :] = zpad

    l_attn.wait()
    l_proj.wait()
    for rel in (2, 1, 3, 0):
        d2d_s[rel] = dot_nn(attn[...], proj[:, pl.ds(col(rel, sc), W)]).astype(BF16)
    pl.semaphore_wait(barrier, len(peers))
    c_d2d = {rel: send(d2d_s.at[rel], d2d_r.at[rel], sibling) for rel in (2, 1, 3, 0)}
    c_yr = {}
    for rel in (2, 1, 3):
        part = dot_nn(attn[...], proj[:, pl.ds(col(rel, c), W)])
        c_d2d[rel].wait_recv()
        ys[rel - 1] = (part + d2d_r[rel].astype(F32)).astype(BF16)
        c_yr[rel] = send(ys.at[rel - 1], yr.at[rel - 1], dev(yy=at_y(rel)))
    part = dot_nn(attn[...], proj[:, pl.ds(col(0, c), W)])
    c_d2d[0].wait_recv()
    l_resid.wait()
    own_acc[...] = part + d2d_r[0].astype(F32) + resid[...].astype(F32)

    l_routes.wait()
    experts = NX * NZ * 2
    row = lax.broadcasted_iota(jnp.int32, (experts, T), 0)
    alive = lax.broadcasted_iota(jnp.int32, (experts, T), 1) < live_ref[0]
    wanted = 2 * ((row & 3) * NZ + (row >> 3)) + ((row >> 2) & 1)
    chosen = row == routes[0:1, :]
    named = wanted == routes[0:1, :]
    for k in range(1, routes.shape[0]):
        chosen = chosen | (row == routes[k : k + 1, :])
        named = named | (wanted == routes[k : k + 1, :])
    act_t = jnp.where(named & alive, 1.0, 0.0)
    before = jnp.where(
        lax.broadcasted_iota(jnp.int32, (T, T), 0) < lax.broadcasted_iota(jnp.int32, (T, T), 1), 1.0, 0.0
    ).astype(BF16)
    position = dot_nn(act_t.astype(BF16), before)
    code[...] = jnp.where(act_t > 0.5, position, -1.0)
    c_code = {}
    for k in range(1, NZ):
        c_code[k] = send(
            code.at[pl.ds(pl.multiple_of(at_z(k) * 8, 8), 8)], cz.at[k], dev(zz=at_z(k))
        )
    cz[0] = code[pl.ds(pl.multiple_of(z * 8, 8), 8), :]

    for rel in (1, 3, 2):
        c_yr[rel].wait_recv()
    total = own_acc[...]
    for k in range(3):
        total = total + yr[k].astype(F32)
    st[0] = total.astype(BF16)
    ones = jnp.ones((8, W), F32)

    def squares(v):
        return lax.dot_general(
            ones, v * v, (((1,), (1,)), ((), ())), precision=lax.Precision.HIGHEST, preferred_element_type=F32
        )

    def share(src, dst):
        sent = []
        for k in (2, 1, 3):
            sent.append(send(src, dst.at[k], dev(yy=at_y(k))))
            sent.append(send(src, dst.at[3 + k], dev(yy=at_y(k), cc=sc)))
        sent.append(send(src, dst.at[0], sibling))
        return sent

    def inverse(sent, src, dst):
        for cp in sent:
            cp.wait_recv()
        tot = src[...]
        for k in range(7):
            tot = tot + dst[k]
        return jnp.transpose(lax.rsqrt(tot / (8 * W) + EPS))[:, 0:1]

    ss_s[...] = squares(st[0].astype(F32))
    c_ss = share(ss_s, ss_r)
    c_st = {rel: send(st.at[0], st.at[rel], dev(yy=at_y(NY - rel))) for rel in (1, 3, 2)}
    l_gain.wait()
    l_ngain.wait()
    gain[...] = gain1[...].reshape(8, W)
    ngain[...] = ngain1[...].reshape(8, W)
    inv = inverse(c_ss, ss_s, ss_r)

    def gain_row(ref, rel):
        return ref[pl.ds(at_y(rel) * 2 + c, 1), :]

    z_right, z_left = dev(zz=at_z(1)), dev(zz=at_z(NZ - 1))
    y_up, y_down = dev(yy=at_y(1)), dev(yy=at_y(NY - 1))
    ring = {}
    yfw = {}
    for rel in (0, 1, 3, 2):
        if rel > 0:
            c_st[rel].wait_recv()
        nb[0, rel] = (st[rel].astype(F32) * inv * gain_row(gain, rel)).astype(BF16)
        if rel < 2:
            ring["R", 0, rel] = send(nb.at[0, rel], nb.at[1, rel], z_right)
            ring["L", 0, rel] = send(nb.at[0, rel], nb.at[NZ - 1, rel], z_left)
    c_sib = send(nb.at[0], nsib, sibling)

    def ring_step(s):
        for way, got, nxt in (("R", s + 1, s + 2), ("L", NZ - 1 - s, NZ - 2 - s)):
            for ch in (0, 1):
                if s == 3 and ch != (0 if way == "R" else 1):
                    continue
                ring[way, s, ch].wait_recv()
                if s < 2 or (s == 2 and ch == (0 if way == "R" else 1)):
                    ring[way, s + 1, ch] = send(
                        nb.at[got, ch], nb.at[nxt, ch], z_right if way == "R" else z_left
                    )
                if ch == 0:
                    yfw[got, 3] = send(nb.at[got, 0], nb.at[got, 3], y_up)
                else:
                    yfw[got, 2] = send(nb.at[got, 1], nb.at[got, 2], y_down)

    slot2 = lax.broadcasted_iota(jnp.int32, (CAP, T), 0).astype(F32)
    slot1 = lax.broadcasted_iota(jnp.int32, (CAP_PAD, T), 0).astype(F32)
    none = jnp.zeros((CAP, T), F32)

    def code_row(ref, k, xp):
        return ref[k, pl.ds(grp * 4 + xp, 1), :]

    def build_slots(p):
        pm = chunk(pmat2, pmat1, p)
        for k in BLOCKS[p]:
            if k > 0:
                c_code[k].wait_recv()
        R = per_owner(p)
        for xp in range(NX):
            if len(BLOCKS[p]) == 2:
                a, b = BLOCKS[p]
                pa = jnp.where(slot2 == code_row(cz, a, xp), 1.0, 0.0)
                pb_ = jnp.where(slot2 == code_row(cz, b, xp), 1.0, 0.0)
                block = jnp.concatenate(
                    [jnp.concatenate([pa, none], axis=1), jnp.concatenate([none, pb_], axis=1)], axis=0
                )
            else:
                block = jnp.where(slot1 == code_row(cz, BLOCKS[p][0], xp), 1.0, 0.0)
            pm[xp * R : (xp + 1) * R, :] = block.astype(BF16)

    def build_weights(p):
        pm, wm = chunk(pmat2, pmat1, p), chunk(wmat2, wmat1, p)
        for k in BLOCKS[p]:
            if k > 0:
                c_gate[k].wait_recv()
        R = per_owner(p)
        parts = []
        for xp in range(NX):
            g = jnp.concatenate([code_row(gz, k, xp) for k in BLOCKS[p]], axis=1)
            parts.append(pm[xp * R : (xp + 1) * R, :].astype(F32) * g)
        wm[...] = jnp.transpose(jnp.concatenate(parts, axis=0)).astype(BF16)

    c_x = {}
    l_x = {}

    def owner_rows(k, p):
        R = per_owner(p)
        return pl.ds(pl.multiple_of(at_x(k) * R, 16), R)

    def slots(p):
        pm, xs, rows = chunk(pmat2, pmat1, p), chunk(xs2, xs1, p), chunk(rows2, rows1, p)
        for rel in range(4):
            picked = None
            for i, k in enumerate(BLOCKS[p]):
                t = dot_nn(pm[:, i * T : (i + 1) * T], nb[k, rel])
                picked = t if picked is None else picked + t
            xs[:, rel * W : (rel + 1) * W] = picked.astype(BF16)
        for k in (2, 1, 3):
            c_x[p, k] = send(xs.at[owner_rows(k, p)], rows.at[owner_rows(0, p)], dev(xx=at_x(k)))
        l_x[p] = local(xs.at[owner_rows(0, p)], rows.at[owner_rows(0, p)])

    c_fw = {}

    def forward(p):
        l_x[p].wait()
        for k in (1, 3, 2):
            c_x[p, k].wait_recv()
        c_fw[p] = send(chunk(rows2, rows1, p), chunk(rsib2, rsib1, p), sibling)

    def swiglu(m, own, sib, weights):
        def up(n, carry):
            units = pl.ds(pl.multiple_of(n * 256, 256), 256)
            acc = None
            for rel in range(4):
                t = dot_nt(own(rel), weights[units, pl.ds(col(rel, c), W)])
                acc = t if acc is None else acc + t
            for rel in range(4):
                acc = acc + dot_nt(sib(rel), weights[units, pl.ds(col(rel, sc), W)])
            gbuf[0:m, units] = acc
            return carry

        lax.fori_loop(0, 2 * FFP // 256, up, 0)

        def act(i, carry):
            part = pl.ds(pl.multiple_of(i * (m // 4), 16), m // 4)
            gate = gbuf[part, 0:FFP]
            hbuf[part, :] = (gate / (1.0 + jnp.exp(-gate)) * gbuf[part, FFP : 2 * FFP]).astype(BF16)
            return carry

        lax.fori_loop(0, 4, act, 0)

    c_t = {}

    def expert(p):
        rows, rsib = chunk(rows2, rows1, p), chunk(rsib2, rsib1, p)
        tsnd, town = chunk(tsnd2, tsnd1, p), chunk(town2, town1, p)
        m = NX * per_owner(p)
        c_fw[p].wait_recv()
        swiglu(
            m,
            lambda rel: rows[:, rel * W : (rel + 1) * W],
            lambda rel: rsib[:, rel * W : (rel + 1) * W],
            gu,
        )
        for rel in range(4):
            t = dot_nn(hbuf[0:m, :], dn[:, pl.ds(col(rel, sc), W)])
            tsnd[:, rel * W : (rel + 1) * W] = t.astype(BF16)
        c_t[p] = send(tsnd, chunk(trcv2, trcv1, p), sibling)
        for rel in range(4):
            t = dot_nn(hbuf[0:m, :], dn[:, pl.ds(col(rel, c), W)])
            town[:, rel * W : (rel + 1) * W] = t.astype(BF16)

    c_ret = {}
    l_ret = {}

    def give_back(p):
        town, rt = chunk(town2, town1, p), chunk(rt2, rt1, p)
        c_t[p].wait_recv()
        town[...] = (town[...].astype(F32) + chunk(trcv2, trcv1, p)[...].astype(F32)).astype(BF16)
        for k in (2, 1, 3):
            c_ret[p, k] = send(town.at[owner_rows(k, p)], rt.at[owner_rows(0, p)], dev(xx=at_x(k)))
        l_ret[p] = local(town.at[owner_rows(0, p)], rt.at[owner_rows(0, p)])

    c_y = {}

    def combine(p):
        wm, rt = chunk(wmat2, wmat1, p), chunk(rt2, rt1, p)
        l_ret[p].wait()
        for k in (1, 3, 2):
            c_ret[p, k].wait_recv()
        for rel in (2, 3, 1, 0):
            for i, k in enumerate(BLOCKS[p]):
                got = dot_nn(wm[i * T : (i + 1) * T, :], rt[:, rel * W : (rel + 1) * W])
                if k == 0:
                    got = got + sh_own[rel] + sh_r[rel].astype(F32)
                if rel < 2:
                    pb[k, rel] = got
                elif rel == 2:
                    ysnd[k, 0] = got.astype(BF16)
                    c_y[k, 1] = send(ysnd.at[k, 0], yrcv.at[k, 1], y_up)
                else:
                    ysnd[k, 1] = got.astype(BF16)
                    c_y[k, 0] = send(ysnd.at[k, 1], yrcv.at[k, 0], y_down)

    build_slots(0)
    slots(0)
    l_router.wait()
    c_sib.wait_recv()
    logits = None
    for rel in range(4):
        t = dot_nt(router[:, pl.ds(col(rel, c), W)], nb[0, rel])
        t = t + dot_nt(router[:, pl.ds(col(rel, sc), W)], nsib[rel])
        logits = t if logits is None else logits + t
    scores = jnp.where(chosen, 1.0 / (1.0 + jnp.exp(-logits)), 0.0)
    gates = scores / jnp.sum(scores, axis=0, keepdims=True) * SCALE
    gates = jnp.where(alive, gates, 0.0).astype(BF16)
    sel_r = lax.broadcasted_iota(jnp.int32, (experts, experts), 0)
    sel_c = lax.broadcasted_iota(jnp.int32, (experts, experts), 1)
    sel_w = 2 * ((sel_r & 3) * NZ + (sel_r >> 3)) + ((sel_r >> 2) & 1)
    gt[...] = dot_nn(jnp.where(sel_c == sel_w, 1.0, 0.0).astype(BF16), gates)
    c_gate = {}
    for k in range(1, NZ):
        c_gate[k] = send(gt.at[pl.ds(pl.multiple_of(at_z(k) * 8, 8), 8)], gz.at[k], dev(zz=at_z(k)))
    gz[0] = gt[pl.ds(pl.multiple_of(z * 8, 8), 8), :]

    def wait_y(p):
        for k in BLOCKS[p]:
            yfw[k, 2].wait_recv()
            yfw[k, 3].wait_recv()

    for p in (1, 2, 3, 4):
        build_slots(p)
    ring_step(0)
    l_sg.wait()
    l_su.wait()
    l_sd.wait()
    swiglu(T, lambda rel: nb[0, rel], lambda rel: nsib[rel], sgu)
    for rel in range(4):
        sh_s[rel] = dot_nn(hbuf[0:T, :], sdn[:, pl.ds(col(rel, sc), W)]).astype(BF16)
    c_sh = send(sh_s, sh_r, sibling)
    for rel in range(4):
        sh_own[rel] = dot_nn(hbuf[0:T, :], sdn[:, pl.ds(col(rel, c), W)])
    forward(0)
    wait_y(1)
    slots(1)
    ring_step(1)
    for p in (0, 1):
        build_weights(p)
    wait_y(2)
    slots(2)
    l_g.wait()
    l_u.wait()
    l_d.wait()
    expert(0)
    ring_step(2)
    forward(1)
    wait_y(3)
    slots(3)
    expert(1)
    ring_step(3)
    wait_y(4)
    slots(4)
    give_back(0)
    forward(2)
    for p in (2, 3, 4):
        build_weights(p)
    expert(2)
    forward(3)
    expert(3)
    forward(4)
    expert(4)
    give_back(4)
    give_back(3)
    give_back(2)
    give_back(1)
    c_sh.wait_recv()
    combine(0)

    back = {}

    def value(k, ch):
        c_y[k, ch].wait_recv()
        return pb[k, ch] + yrcv[k, ch].astype(F32)

    def pass_on(wi, way, s, ch, k, to):
        v = value(k, ch)
        if (way, s - 1, ch) in back:
            back[way, s - 1, ch].wait_recv()
            v = v + rs_r[wi, s - 1, ch].astype(F32)
        rs_s[wi, s, ch] = v.astype(BF16)
        back[way, s, ch] = send(rs_s.at[wi, s, ch], rs_r.at[wi, s, ch], to)

    combine(4)
    pass_on(0, "L", 0, 0, 4, z_left)
    pass_on(1, "R", 0, 1, 4, z_right)
    for s in (1, 2, 3):
        combine(4 - s)
        for ch in (1, 0):
            pass_on(0, "L", s, ch, 4 - s, z_left)
            pass_on(1, "R", s, ch, 4 + s, z_right)

    def finish(ch):
        v = value(0, ch)
        for wi, way in ((0, "L"), (1, "R")):
            back[way, 3, ch].wait_recv()
            v = v + rs_r[wi, 3, ch].astype(F32)
        return v

    fb_s[...] = finish(1).astype(BF16)
    c_fb = send(fb_s, fb_r, y_up)
    mine = finish(0) + st[0].astype(F32)
    c_fb.wait_recv()
    nxt = (mine + fb_r[...].astype(F32)).astype(BF16)
    out_s[...] = nxt
    wide = nxt.astype(F32)
    q_s[...] = squares(wide)
    inv2 = inverse(share(q_s, q_r), q_s, q_r)
    out_n[...] = (wide * inv2 * gain_row(ngain, 0)).astype(BF16)
    for cp in copies:
        cp.wait_send()


N_SEND = 192


def on_device(
    attn_out, out_proj, residual, norm_gain, router, expert_gate_up, expert_down,
    shared_gate_up, shared_down, routes, live_rows, next_gain,
):
    T, W = attn_out.shape
    D = out_proj.shape[1]
    FF = expert_down.shape[1]
    FFP = -(-FF // 128) * 128
    H = D // 2
    R2, R1 = NX * 2 * CAP, NX * CAP_PAD
    fanout = routes.shape[1]
    vm = pltpu.VMEM
    both = [vm((3, R2, H), BF16), vm((2, R1, H), BF16)]
    scratch = [
        vm((T, W), BF16), vm((W, D), BF16), vm((T, W), BF16), vm((D,), F32), vm((8, W), F32), vm((64, D), BF16),
        vm((2 * FFP, D), BF16), vm((FFP, D), BF16), vm((2 * FFP, D), BF16), vm((FFP, D), BF16),
        vm((fanout, T), jnp.int32), vm((D,), F32), vm((8, W), F32),
        vm((4, T, W), BF16), vm((4, T, W), BF16), vm((3, T, W), BF16), vm((3, T, W), BF16),
        vm((4, T, W), BF16), vm((T, W), F32), vm((8, T), F32), vm((7, 8, T), F32),
        vm((64, T), F32), vm((NZ, 8, T), F32), vm((64, T), F32), vm((NZ, 8, T), F32),
        vm((NZ, 4, T, W), BF16), vm((4, T, W), BF16),
        vm((3, R2, 2 * T), BF16), vm((2, R1, T), BF16), vm((3, 2 * T, R2), BF16), vm((2, T, R1), BF16),
        *both, *both, *both,
        vm((R2, 2 * FFP), F32), vm((R2, FFP), BF16),
        *both, *both, *both, *both,
        vm((4, T, W), F32), vm((4, T, W), BF16), vm((4, T, W), BF16),
        vm((NZ, 2, T, W), F32), vm((NZ, 2, T, W), BF16), vm((NZ, 2, T, W), BF16),
        vm((2, 4, 2, T, W), BF16), vm((2, 4, 2, T, W), BF16),
        vm((T, W), BF16), vm((T, W), BF16), vm((8, T), F32), vm((7, 8, T), F32),
        pltpu.SemaphoreType.DMA((13,)), pltpu.SemaphoreType.DMA((10,)),
        pltpu.SemaphoreType.DMA((N_SEND,)), pltpu.SemaphoreType.DMA((N_SEND,)),
    ]
    hbm = pl.BlockSpec(memory_space=pl.ANY)
    return pl.pallas_call(
        kernel,
        out_shape=(jax.ShapeDtypeStruct((T, W), BF16), jax.ShapeDtypeStruct((T, W), BF16)),
        in_specs=[pl.BlockSpec(memory_space=pltpu.SMEM)] + [hbm] * 11,
        out_specs=(pl.BlockSpec(memory_space=pltpu.VMEM), pl.BlockSpec(memory_space=pltpu.VMEM)),
        scratch_shapes=scratch,
        compiler_params=pltpu.CompilerParams(
            collective_id=0, has_side_effects=True, vmem_limit_bytes=67043328
        ),
    )(
        live_rows, attn_out, out_proj, residual, norm_gain, router.T, expert_gate_up,
        expert_down, shared_gate_up, shared_down, routes.T, next_gain,
    )


def solution(mesh):
    in_specs = (
        P("ep", "tp"),
        P("tp", None),
        P("ep", None),
        P(),
        P(),
        P(("ep", "tp"), None, None, None),
        P(("ep", "tp"), None, None),
        P(None, "tp", None),
        P("tp", None),
        P("ep", None),
        P("ep"),
        P(),
    )
    out_specs = (P("ep", "tp"), P("ep", "tp"))
    return jax.shard_map(
        on_device, mesh=mesh, in_specs=in_specs, out_specs=out_specs, check_vma=False
    )
```

```python
import jax
import jax.numpy as jnp
from jax import lax
from jax.experimental import pallas as pl
from jax.experimental.pallas import tpu as pltpu
from jax.sharding import PartitionSpec as P

NX, NZ, NY = 4, 8, 4
CAP = 40
CAP_PAD = 48
BLOCKS = {0: (0,), 1: (1, 7), 2: (2, 6), 3: (3, 5), 4: (4,)}
EPS = 1e-06
SCALE = 2.446
F32 = jnp.float32
BF16 = jnp.bfloat16
MESH = pl.DeviceIdType.MESH


def dot_nn(a, b):
    return lax.dot_general(a, b, (((1,), (0,)), ((), ())), preferred_element_type=F32)


def dot_nt(a, b):
    return lax.dot_general(a, b, (((1,), (1,)), ((), ())), preferred_element_type=F32)


def dot_tn(a, b):
    return lax.dot_general(a, b, (((0,), (0,)), ((), ())), preferred_element_type=F32)


def kernel(
    live_ref, attn_h, proj_h, resid_h, gain_h, router_h, gu_h, dn_h, sgu_h, sdn_h, routes_h, ngain_h,
    out_s, out_n,
    attn, proj, resid, gain1, gain, router, gu, dn, sgu, sdn, routes, ngain1, ngain,
    d2d_s, d2d_r, ys, yr, st, own_acc, ss_s, ss_r,
    code, cz, gt, gz,
    nb, nsib, pmat2, pmat1, wmat2, wmat1, xs2, xs1, rows2, rows1, rsib2, rsib1,
    gbuf, hbuf, tsnd2, tsnd1, trcv2, trcv1, town2, town1, rt2, rt1,
    sh_own, sh_s, sh_r,
    pb, ysnd, yrcv, rs_s, rs_r, fb_s, fb_r, q_s, q_r,
    load_sem, local_sem, send_sem, recv_sem,
):
    ep = lax.axis_index("ep")
    tp = lax.axis_index("tp")
    x, z = ep // NZ, lax.rem(ep, NZ)
    y, c = tp // 2, lax.rem(tp, 2)
    grp = y // 2
    sc = 1 - c
    T = attn.shape[0]
    W = attn.shape[1]
    FFP = gu.shape[0] // 2
    FF = gu_h.shape[2]

    def chunk(double, single, p):
        return double.at[p - 1] if 1 <= p <= 3 else single.at[p // 4]

    def per_owner(p):
        return 2 * CAP if 1 <= p <= 3 else CAP_PAD

    def at_y(k):
        return lax.rem(y + k, NY)

    def at_z(k):
        return lax.rem(z + k, NZ)

    def at_x(k):
        return lax.rem(x + k, NX)

    def dev(xx=None, zz=None, yy=None, cc=None):
        xx = x if xx is None else xx
        zz = z if zz is None else zz
        yy = y if yy is None else yy
        cc = c if cc is None else cc
        return (xx * NZ + zz, yy * 2 + cc)

    sibling = dev(cc=sc)

    def col(rel, core):
        return pl.multiple_of((at_y(rel) * 2 + core) * W, W)

    copies = []
    fresh = iter(range(N_RECV))

    def group():
        return next(fresh)

    def send(src, dst, to, sem=None):
        i = len(copies)
        if i >= N_SEND:
            copies[i - N_SEND].wait_send()
        cp = pltpu.make_async_remote_copy(
            src_ref=src, dst_ref=dst, send_sem=send_sem.at[i % N_SEND],
            recv_sem=recv_sem.at[group() if sem is None else sem], device_id=to, device_id_type=MESH,
        )
        cp.start()
        copies.append(cp)
        return cp

    def arrived(sem, size):
        pltpu.make_async_remote_copy(
            src_ref=size, dst_ref=size, send_sem=send_sem.at[0], recv_sem=recv_sem.at[sem],
            device_id=sibling, device_id_type=MESH,
        ).wait_recv()

    loads = []

    def load(src, dst):
        i = len(loads)
        cp = pltpu.make_async_copy(src, dst, load_sem.at[i])
        cp.start()
        loads.append(cp)
        return cp

    locals_ = []

    def local(src, dst):
        i = len(locals_)
        cp = pltpu.make_async_copy(src, dst, local_sem.at[i])
        cp.start()
        locals_.append(cp)
        return cp

    l_attn = load(attn_h, attn)
    l_proj = load(proj_h, proj)
    l_routes = load(routes_h, routes)
    l_resid = load(resid_h.at[:, pl.ds(col(0, c), W)], resid)
    l_gain = load(gain_h, gain1)
    l_ngain = load(ngain_h, ngain1)
    l_router = load(router_h, router)
    l_sg = load(sgu_h.at[0], sgu.at[pl.ds(0, FF)])
    l_su = load(sgu_h.at[1], sgu.at[pl.ds(FFP, FF)])
    l_sd = load(sdn_h, sdn.at[pl.ds(0, FF)])
    l_g = load(gu_h.at[0, 0], gu.at[pl.ds(0, FF)])
    l_u = load(gu_h.at[0, 1], gu.at[pl.ds(FFP, FF)])
    l_d = load(dn_h.at[0], dn.at[pl.ds(0, FF)])

    peers = [sibling]
    peers += [dev(yy=at_y(k)) for k in (1, 2, 3)]
    peers += [dev(yy=at_y(k), cc=sc) for k in (1, 2, 3)]
    peers += [dev(xx=at_x(k)) for k in (1, 2, 3)]
    peers += [dev(zz=at_z(k)) for k in range(1, NZ)]
    barrier = pltpu.get_barrier_semaphore()
    for peer in peers:
        pl.semaphore_signal(barrier, inc=1, device_id=peer, device_id_type=MESH)

    zpad = jnp.zeros((FFP - FF, gu.shape[1]), BF16)
    for ref in (gu, sgu):
        ref[FF:FFP, :] = zpad
        ref[FFP + FF : 2 * FFP, :] = zpad
    for ref in (dn, sdn):
        ref[FF:FFP, :] = zpad

    l_attn.wait()
    l_proj.wait()
    for rel in (2, 1, 3, 0):
        d2d_s[rel] = dot_nn(attn[...], proj[:, pl.ds(col(rel, sc), W)]).astype(BF16)
    pl.semaphore_wait(barrier, len(peers))
    c_d2d = {rel: send(d2d_s.at[rel], d2d_r.at[rel], sibling) for rel in (2, 1, 3, 0)}
    c_yr = {}
    for rel in (2, 1, 3):
        part = dot_nn(attn[...], proj[:, pl.ds(col(rel, c), W)])
        c_d2d[rel].wait_recv()
        ys[rel - 1] = (part + d2d_r[rel].astype(F32)).astype(BF16)
        c_yr[rel] = send(ys.at[rel - 1], yr.at[rel - 1], dev(yy=at_y(rel)))
    part = dot_nn(attn[...], proj[:, pl.ds(col(0, c), W)])
    c_d2d[0].wait_recv()
    l_resid.wait()
    own_acc[...] = part + d2d_r[0].astype(F32) + resid[...].astype(F32)

    l_routes.wait()
    experts = NX * NZ * 2
    row = lax.broadcasted_iota(jnp.int32, (experts, T), 0)
    alive = lax.broadcasted_iota(jnp.int32, (experts, T), 1) < live_ref[0]
    wanted = 2 * ((row & 3) * NZ + (row >> 3)) + ((row >> 2) & 1)
    chosen = row == routes[0:1, :]
    named = wanted == routes[0:1, :]
    for k in range(1, routes.shape[0]):
        chosen = chosen | (row == routes[k : k + 1, :])
        named = named | (wanted == routes[k : k + 1, :])
    act_t = jnp.where(named & alive, 1.0, 0.0)
    before = jnp.where(
        lax.broadcasted_iota(jnp.int32, (T, T), 0) < lax.broadcasted_iota(jnp.int32, (T, T), 1), 1.0, 0.0
    ).astype(BF16)
    position = dot_nn(act_t.astype(BF16), before)
    code[...] = jnp.where(act_t > 0.5, position, -1.0)
    s_code = group()
    for k in range(1, NZ):
        send(code.at[pl.ds(pl.multiple_of(at_z(k) * 8, 8), 8)], cz.at[k], dev(zz=at_z(k)), s_code)
    cz[0] = code[pl.ds(pl.multiple_of(z * 8, 8), 8), :]

    for rel in (1, 3, 2):
        c_yr[rel].wait_recv()
    total = own_acc[...]
    for k in range(3):
        total = total + yr[k].astype(F32)
    st[0] = total.astype(BF16)
    ones = jnp.ones((8, W), F32)

    def squares(v):
        return lax.dot_general(
            ones, v * v, (((1,), (1,)), ((), ())), precision=lax.Precision.HIGHEST, preferred_element_type=F32
        )

    def share(src, dst):
        sem = group()
        for k in (2, 1, 3):
            send(src, dst.at[k], dev(yy=at_y(k)), sem)
            send(src, dst.at[3 + k], dev(yy=at_y(k), cc=sc), sem)
        send(src, dst.at[0], sibling, sem)
        return sem

    def inverse(sem, src, dst):
        arrived(sem, dst)
        tot = src[...]
        for k in range(7):
            tot = tot + dst[k]
        return jnp.transpose(lax.rsqrt(tot / (8 * W) + EPS))[:, 0:1]

    ss_s[...] = squares(st[0].astype(F32))
    c_ss = share(ss_s, ss_r)
    c_st = {rel: send(st.at[0], st.at[rel], dev(yy=at_y(NY - rel))) for rel in (1, 3, 2)}
    l_gain.wait()
    l_ngain.wait()
    gain[...] = gain1[...].reshape(8, W)
    ngain[...] = ngain1[...].reshape(8, W)
    slot1 = lax.broadcasted_iota(jnp.int32, (CAP_PAD, T), 0).astype(F32)
    for xp in range(NX):
        own_code = cz[0, pl.ds(grp * 4 + xp, 1), :]
        pmat1[0, xp * CAP_PAD : (xp + 1) * CAP_PAD, :] = jnp.where(slot1 == own_code, 1.0, 0.0).astype(BF16)
    inv = inverse(c_ss, ss_s, ss_r)

    def gain_row(ref, rel):
        return ref[pl.ds(at_y(rel) * 2 + c, 1), :]

    z_right, z_left = dev(zz=at_z(1)), dev(zz=at_z(NZ - 1))
    y_up, y_down = dev(yy=at_y(1)), dev(yy=at_y(NY - 1))
    ring = {}
    yfw = {}

    def normalise(rel):
        if rel > 0:
            c_st[rel].wait_recv()
        nb[0, rel] = (st[rel].astype(F32) * inv * gain_row(gain, rel)).astype(BF16)
        if rel < 2:
            ring["R", 0, rel] = send(nb.at[0, rel], nb.at[1, rel], z_right)
            ring["L", 0, rel] = send(nb.at[0, rel], nb.at[NZ - 1, rel], z_left)

    normalise(0)
    normalise(1)

    s_yfw = {p: group() for p in (1, 2, 3, 4)}

    def ring_step(s):
        for ch in (0, 1):
            for way, got, nxt in (("R", s + 1, s + 2), ("L", NZ - 1 - s, NZ - 2 - s)):
                if s == 3 and ch != (0 if way == "R" else 1):
                    continue
                ring[way, s, ch].wait_recv()
                if s < 2 or (s == 2 and ch == (0 if way == "R" else 1)):
                    ring[way, s + 1, ch] = send(
                        nb.at[got, ch], nb.at[nxt, ch], z_right if way == "R" else z_left
                    )
                if ch == 0:
                    send(nb.at[got, 0], nb.at[got, 3], y_up, s_yfw[s + 1])
                else:
                    send(nb.at[got, 1], nb.at[got, 2], y_down, s_yfw[s + 1])

    slot2 = lax.broadcasted_iota(jnp.int32, (CAP, T), 0).astype(F32)
    slot1 = lax.broadcasted_iota(jnp.int32, (CAP_PAD, T), 0).astype(F32)
    none = jnp.zeros((CAP, T), F32)

    def code_row(ref, k, xp):
        return ref[k, pl.ds(grp * 4 + xp, 1), :]

    def build_slots(p):
        pm = chunk(pmat2, pmat1, p)
        R = per_owner(p)
        for xp in range(NX):
            if len(BLOCKS[p]) == 2:
                a, b = BLOCKS[p]
                pa = jnp.where(slot2 == code_row(cz, a, xp), 1.0, 0.0)
                pb_ = jnp.where(slot2 == code_row(cz, b, xp), 1.0, 0.0)
                block = jnp.concatenate(
                    [jnp.concatenate([pa, none], axis=1), jnp.concatenate([none, pb_], axis=1)], axis=0
                )
            else:
                block = jnp.where(slot1 == code_row(cz, BLOCKS[p][0], xp), 1.0, 0.0)
            pm[xp * R : (xp + 1) * R, :] = block.astype(BF16)

    def build_weights(p):
        pm, wm = chunk(pmat2, pmat1, p), chunk(wmat2, wmat1, p)
        R = per_owner(p)
        parts = []
        for xp in range(NX):
            g = jnp.concatenate([code_row(gz, k, xp) for k in BLOCKS[p]], axis=1)
            parts.append(pm[xp * R : (xp + 1) * R, :].astype(F32) * g)
        wm[...] = jnp.transpose(jnp.concatenate(parts, axis=0)).astype(BF16)

    s_x = {p: group() for p in range(5)}
    l_x = {}

    def owner_rows(k, p):
        R = per_owner(p)
        return pl.ds(pl.multiple_of(at_x(k) * R, 16), R)

    def slots(p, half):
        pm, xs, rows = chunk(pmat2, pmat1, p), chunk(xs2, xs1, p), chunk(rows2, rows1, p)
        for rel in (2 * half, 2 * half + 1):
            picked = None
            for i, k in enumerate(BLOCKS[p]):
                t = dot_nn(pm[:, i * T : (i + 1) * T], nb[k, rel])
                picked = t if picked is None else picked + t
            xs[:, rel * W : (rel + 1) * W] = picked.astype(BF16)
        cols = pl.ds(2 * half * W, 2 * W)
        for k in (2, 1, 3):
            send(xs.at[owner_rows(k, p), cols], rows.at[owner_rows(0, p), cols], dev(xx=at_x(k)), s_x[p])
        if half == 1:
            l_x[p] = local(xs.at[owner_rows(0, p)], rows.at[owner_rows(0, p)])

    c_fw = {}

    def forward(p):
        rows = chunk(rows2, rows1, p)
        l_x[p].wait()
        arrived(s_x[p], rows.at[pl.ds(0, 3 * per_owner(p))])
        c_fw[p] = send(rows, chunk(rsib2, rsib1, p), sibling)

    def swiglu(m, own, sib, weights):
        def up(n, carry):
            units = pl.ds(pl.multiple_of(n * 256, 256), 256)
            acc = None
            for rel in range(4):
                t = dot_nt(own(rel), weights[units, pl.ds(col(rel, c), W)])
                acc = t if acc is None else acc + t
            for rel in range(4):
                acc = acc + dot_nt(sib(rel), weights[units, pl.ds(col(rel, sc), W)])
            gbuf[0:m, units] = acc
            return carry

        lax.fori_loop(0, 2 * FFP // 256, up, 0)

        def act(i, carry):
            part = pl.ds(pl.multiple_of(i * (m // 4), 16), m // 4)
            gate = gbuf[part, 0:FFP]
            hbuf[part, :] = (gate / (1.0 + jnp.exp(-gate)) * gbuf[part, FFP : 2 * FFP]).astype(BF16)
            return carry

        lax.fori_loop(0, 4, act, 0)

    c_t = {}

    def expert(p):
        rows, rsib = chunk(rows2, rows1, p), chunk(rsib2, rsib1, p)
        tsnd, town = chunk(tsnd2, tsnd1, p), chunk(town2, town1, p)
        m = NX * per_owner(p)
        c_fw[p].wait_recv()
        swiglu(
            m,
            lambda rel: rows[:, rel * W : (rel + 1) * W],
            lambda rel: rsib[:, rel * W : (rel + 1) * W],
            gu,
        )
        for rel in range(4):
            t = dot_nn(hbuf[0:m, :], dn[:, pl.ds(col(rel, sc), W)])
            tsnd[:, rel * W : (rel + 1) * W] = t.astype(BF16)
        c_t[p] = send(tsnd, chunk(trcv2, trcv1, p), sibling)
        for rel in range(4):
            t = dot_nn(hbuf[0:m, :], dn[:, pl.ds(col(rel, c), W)])
            town[:, rel * W : (rel + 1) * W] = t.astype(BF16)

    s_ret = {}
    l_ret = {}

    def give_back(p):
        town, rt = chunk(town2, town1, p), chunk(rt2, rt1, p)
        trcv = chunk(trcv2, trcv1, p)
        c_t[p].wait_recv()
        for half in (1, 0):
            cols = slice(2 * half * W, 2 * (half + 1) * W)
            window = pl.ds(2 * half * W, 2 * W)
            town[:, cols] = (town[:, cols].astype(F32) + trcv[:, cols].astype(F32)).astype(BF16)
            s_ret[p, half] = group()
            for k in (2, 1, 3):
                send(
                    town.at[owner_rows(k, p), window], rt.at[owner_rows(0, p), window],
                    dev(xx=at_x(k)), s_ret[p, half],
                )
        l_ret[p] = local(town.at[owner_rows(0, p)], rt.at[owner_rows(0, p)])

    c_y = {}

    def combine(p):
        wm, rt = chunk(wmat2, wmat1, p), chunk(rt2, rt1, p)
        l_ret[p].wait()
        for rel in (2, 3, 1, 0):
            if rel in (1, 2):
                half = rel // 2
                arrived(s_ret[p, half], rt.at[pl.ds(0, 3 * per_owner(p)), pl.ds(2 * half * W, 2 * W)])
            order = list(enumerate(BLOCKS[p]))
            for i, k in order if rel in (2, 1) else order[::-1]:
                got = dot_nn(wm[i * T : (i + 1) * T, :], rt[:, rel * W : (rel + 1) * W])
                if k == 0:
                    got = got + sh_own[rel] + sh_r[rel].astype(F32)
                if rel < 2:
                    pb[k, rel] = got
                elif rel == 2:
                    ysnd[k, 0] = got.astype(BF16)
                    c_y[k, 1] = send(ysnd.at[k, 0], yrcv.at[k, 1], y_up)
                else:
                    ysnd[k, 1] = got.astype(BF16)
                    c_y[k, 0] = send(ysnd.at[k, 1], yrcv.at[k, 0], y_down)

    def wait_y(p):
        k = BLOCKS[p][0]
        arrived(s_yfw[p], nb.at[k] if p < 4 else nb.at[k, pl.ds(0, 2)])

    slots(0, 0)
    for rel in (3, 2):
        normalise(rel)
    c_sib = send(nb.at[0], nsib, sibling)
    slots(0, 1)
    arrived(s_code, cz.at[pl.ds(1, NZ - 1)])
    for p in (1, 2, 3, 4):
        build_slots(p)
    l_router.wait()
    c_sib.wait_recv()
    logits = None
    for rel in range(4):
        t = dot_nt(router[:, pl.ds(col(rel, c), W)], nb[0, rel])
        t = t + dot_nt(router[:, pl.ds(col(rel, sc), W)], nsib[rel])
        logits = t if logits is None else logits + t
    scores = jnp.where(chosen, 1.0 / (1.0 + jnp.exp(-logits)), 0.0)
    gates = scores / jnp.sum(scores, axis=0, keepdims=True) * SCALE
    gates = jnp.where(alive, gates, 0.0).astype(BF16)
    sel_r = lax.broadcasted_iota(jnp.int32, (experts, experts), 0)
    sel_c = lax.broadcasted_iota(jnp.int32, (experts, experts), 1)
    sel_w = 2 * ((sel_r & 3) * NZ + (sel_r >> 3)) + ((sel_r >> 2) & 1)
    gt[...] = dot_nn(jnp.where(sel_c == sel_w, 1.0, 0.0).astype(BF16), gates)
    s_gate = group()
    for k in range(1, NZ):
        send(gt.at[pl.ds(pl.multiple_of(at_z(k) * 8, 8), 8)], gz.at[k], dev(zz=at_z(k)), s_gate)
    gz[0] = gt[pl.ds(pl.multiple_of(z * 8, 8), 8), :]

    ring_step(0)
    slots(1, 0)
    forward(0)
    l_sg.wait()
    l_su.wait()
    l_sd.wait()
    swiglu(T, lambda rel: nb[0, rel], lambda rel: nsib[rel], sgu)
    wait_y(1)
    slots(1, 1)
    ring_step(1)
    slots(2, 0)
    for rel in range(4):
        sh_s[rel] = dot_nn(hbuf[0:T, :], sdn[:, pl.ds(col(rel, sc), W)]).astype(BF16)
    c_sh = send(sh_s, sh_r, sibling)
    for rel in range(4):
        sh_own[rel] = dot_nn(hbuf[0:T, :], sdn[:, pl.ds(col(rel, c), W)])
    l_g.wait()
    l_u.wait()
    l_d.wait()
    expert(0)
    wait_y(2)
    slots(2, 1)
    ring_step(2)
    slots(3, 0)
    forward(1)
    ring_step(3)
    wait_y(3)
    slots(3, 1)
    wait_y(4)
    slots(4, 0)
    slots(4, 1)
    give_back(0)
    expert(1)
    forward(2)
    arrived(s_gate, gz.at[pl.ds(1, NZ - 1)])
    for p in range(5):
        build_weights(p)
    expert(2)
    forward(3)
    expert(3)
    forward(4)
    expert(4)
    give_back(4)
    give_back(3)
    give_back(2)
    give_back(1)
    c_sh.wait_recv()
    combine(0)

    back = {}

    def value(k, ch):
        c_y[k, ch].wait_recv()
        return pb[k, ch] + yrcv[k, ch].astype(F32)

    def pass_on(wi, way, s, ch, k, to):
        v = value(k, ch)
        if (way, s - 1, ch) in back:
            back[way, s - 1, ch].wait_recv()
            v = v + rs_r[wi, s - 1, ch].astype(F32)
        rs_s[wi, s, ch] = v.astype(BF16)
        back[way, s, ch] = send(rs_s.at[wi, s, ch], rs_r.at[wi, s, ch], to)

    combine(4)
    pass_on(0, "L", 0, 0, 4, z_left)
    pass_on(1, "R", 0, 1, 4, z_right)
    for s in (1, 2, 3):
        combine(4 - s)
        for ch in (1, 0):
            pass_on(0, "L", s, ch, 4 - s, z_left)
            pass_on(1, "R", s, 1 - ch, 4 + s, z_right)

    def finish(ch):
        v = value(0, ch)
        for wi, way in ((0, "L"), (1, "R")):
            back[way, 3, ch].wait_recv()
            v = v + rs_r[wi, 3, ch].astype(F32)
        return v

    fb_s[...] = finish(1).astype(BF16)
    c_fb = send(fb_s, fb_r, y_up)
    mine = finish(0) + st[0].astype(F32)
    c_fb.wait_recv()
    nxt = (mine + fb_r[...].astype(F32)).astype(BF16)
    out_s[...] = nxt
    wide = nxt.astype(F32)
    q_s[...] = squares(wide)
    inv2 = inverse(share(q_s, q_r), q_s, q_r)
    out_n[...] = (wide * inv2 * gain_row(ngain, 0)).astype(BF16)
    for cp in copies[-N_SEND:]:
        cp.wait_send()


N_SEND = 32
N_RECV = 94


def on_device(
    attn_out, out_proj, residual, norm_gain, router, expert_gate_up, expert_down,
    shared_gate_up, shared_down, routes, live_rows, next_gain,
):
    T, W = attn_out.shape
    D = out_proj.shape[1]
    FF = expert_down.shape[1]
    FFP = -(-FF // 128) * 128
    H = D // 2
    R2, R1 = NX * 2 * CAP, NX * CAP_PAD
    fanout = routes.shape[1]
    vm = pltpu.VMEM
    both = [vm((3, R2, H), BF16), vm((2, R1, H), BF16)]
    scratch = [
        vm((T, W), BF16), vm((W, D), BF16), vm((T, W), BF16), vm((D,), F32), vm((8, W), F32), vm((64, D), BF16),
        vm((2 * FFP, D), BF16), vm((FFP, D), BF16), vm((2 * FFP, D), BF16), vm((FFP, D), BF16),
        vm((fanout, T), jnp.int32), vm((D,), F32), vm((8, W), F32),
        vm((4, T, W), BF16), vm((4, T, W), BF16), vm((3, T, W), BF16), vm((3, T, W), BF16),
        vm((4, T, W), BF16), vm((T, W), F32), vm((8, T), F32), vm((7, 8, T), F32),
        vm((64, T), F32), vm((NZ, 8, T), F32), vm((64, T), F32), vm((NZ, 8, T), F32),
        vm((NZ, 4, T, W), BF16), vm((4, T, W), BF16),
        vm((3, R2, 2 * T), BF16), vm((2, R1, T), BF16), vm((3, 2 * T, R2), BF16), vm((2, T, R1), BF16),
        *both, *both, *both,
        vm((R2, 2 * FFP), F32), vm((R2, FFP), BF16),
        *both, *both, *both, *both,
        vm((4, T, W), F32), vm((4, T, W), BF16), vm((4, T, W), BF16),
        vm((NZ, 2, T, W), F32), vm((NZ, 2, T, W), BF16), vm((NZ, 2, T, W), BF16),
        vm((2, 4, 2, T, W), BF16), vm((2, 4, 2, T, W), BF16),
        vm((T, W), BF16), vm((T, W), BF16), vm((8, T), F32), vm((7, 8, T), F32),
        pltpu.SemaphoreType.DMA((13,)), pltpu.SemaphoreType.DMA((10,)),
        pltpu.SemaphoreType.DMA((N_SEND,)), pltpu.SemaphoreType.DMA((N_RECV,)),
    ]
    hbm = pl.BlockSpec(memory_space=pl.ANY)
    return pl.pallas_call(
        kernel,
        out_shape=(jax.ShapeDtypeStruct((T, W), BF16), jax.ShapeDtypeStruct((T, W), BF16)),
        in_specs=[pl.BlockSpec(memory_space=pltpu.SMEM)] + [hbm] * 11,
        out_specs=(pl.BlockSpec(memory_space=pltpu.VMEM), pl.BlockSpec(memory_space=pltpu.VMEM)),
        scratch_shapes=scratch,
        compiler_params=pltpu.CompilerParams(
            collective_id=0, has_side_effects=True, vmem_limit_bytes=67043328
        ),
    )(
        live_rows, attn_out, out_proj, residual, norm_gain, router.T, expert_gate_up,
        expert_down, shared_gate_up, shared_down, routes.T, next_gain,
    )


def solution(mesh):
    in_specs = (
        P("ep", "tp"),
        P("tp", None),
        P("ep", None),
        P(),
        P(),
        P(("ep", "tp"), None, None, None),
        P(("ep", "tp"), None, None),
        P(None, "tp", None),
        P("tp", None),
        P("ep", None),
        P("ep"),
        P(),
    )
    out_specs = (P("ep", "tp"), P("ep", "tp"))
    return jax.shard_map(
        on_device, mesh=mesh, in_specs=in_specs, out_specs=out_specs, check_vma=False
    )
```

```python
import jax
import jax.numpy as jnp
from jax import lax
from jax.experimental import pallas as pl
from jax.experimental.pallas import tpu as pltpu
from jax.sharding import PartitionSpec as P

NX, NZ, NY = 4, 8, 4
CAP = 40
CAP_PAD = 48
BLOCKS = {0: (0,), 1: (1, 7), 2: (2, 6), 3: (3, 5), 4: (4,)}
EPS = 1e-06
SCALE = 2.446
F32 = jnp.float32
BF16 = jnp.bfloat16
MESH = pl.DeviceIdType.MESH


def dot_nn(a, b):
    return lax.dot_general(a, b, (((1,), (0,)), ((), ())), preferred_element_type=F32)


def dot_nt(a, b):
    return lax.dot_general(a, b, (((1,), (1,)), ((), ())), preferred_element_type=F32)


def dot_tn(a, b):
    return lax.dot_general(a, b, (((0,), (0,)), ((), ())), preferred_element_type=F32)


def kernel(
    live_ref, attn_h, proj_h, resid_h, gain_h, router_h, gu_h, dn_h, sgu_h, sdn_h, routes_h, ngain_h,
    out_s, out_n,
    attn, proj, resid, gain1, gain, router, gu, dn, sgu, sdn, routes, ngain1, ngain,
    d2d_s, d2d_r, ys, yr, st, own_acc, ss_s, ss_r,
    code, cz, gt, gz,
    nb, nsib, pmat2, pmat1, wmat2, wmat1, xs2, xs1, rows2, rows1, rsib2, rsib1,
    gbuf, hbuf, tsnd2, tsnd1, trcv2, trcv1, town2, town1, rt2, rt1,
    sh_own, sh_s, sh_r,
    pb, ysnd, yrcv, rs_s, rs_r, fb_s, fb_r, q_s, q_r,
    load_sem, local_sem, send_sem, recv_sem,
):
    ep = lax.axis_index("ep")
    tp = lax.axis_index("tp")
    x, z = ep // NZ, lax.rem(ep, NZ)
    y, c = tp // 2, lax.rem(tp, 2)
    grp = y // 2
    sc = 1 - c
    T = attn.shape[0]
    W = attn.shape[1]
    FFP = gu.shape[0] // 2
    FF = gu_h.shape[2]

    def chunk(double, single, p):
        return double.at[p - 1] if 1 <= p <= 3 else single.at[p // 4]

    def per_owner(p):
        return 2 * CAP if 1 <= p <= 3 else CAP_PAD

    def at_y(k):
        return lax.rem(y + k, NY)

    def at_z(k):
        return lax.rem(z + k, NZ)

    def at_x(k):
        return lax.rem(x + k, NX)

    def dev(xx=None, zz=None, yy=None, cc=None):
        xx = x if xx is None else xx
        zz = z if zz is None else zz
        yy = y if yy is None else yy
        cc = c if cc is None else cc
        return (xx * NZ + zz, yy * 2 + cc)

    sibling = dev(cc=sc)

    def col(rel, core):
        return pl.multiple_of((at_y(rel) * 2 + core) * W, W)

    copies = []
    fresh = iter(range(N_RECV))

    def group():
        return next(fresh)

    def send(src, dst, to, sem=None):
        i = len(copies)
        if i >= N_SEND:
            copies[i - N_SEND].wait_send()
        cp = pltpu.make_async_remote_copy(
            src_ref=src, dst_ref=dst, send_sem=send_sem.at[i % N_SEND],
            recv_sem=recv_sem.at[group() if sem is None else sem], device_id=to, device_id_type=MESH,
        )
        cp.start()
        copies.append(cp)
        return cp

    def arrived(sem, size):
        pltpu.make_async_remote_copy(
            src_ref=size, dst_ref=size, send_sem=send_sem.at[0], recv_sem=recv_sem.at[sem],
            device_id=sibling, device_id_type=MESH,
        ).wait_recv()

    loads = []

    def load(src, dst):
        i = len(loads)
        cp = pltpu.make_async_copy(src, dst, load_sem.at[i])
        cp.start()
        loads.append(cp)
        return cp

    locals_ = []

    def local(src, dst):
        i = len(locals_)
        cp = pltpu.make_async_copy(src, dst, local_sem.at[i])
        cp.start()
        locals_.append(cp)
        return cp

    l_attn = load(attn_h, attn)
    l_proj = load(proj_h, proj)
    l_routes = load(routes_h, routes)
    l_resid = load(resid_h.at[:, pl.ds(col(0, c), W)], resid)
    l_gain = load(gain_h, gain1)
    l_ngain = load(ngain_h, ngain1)
    l_router = load(router_h, router)
    l_sg = load(sgu_h.at[0], sgu.at[pl.ds(0, FF)])
    l_su = load(sgu_h.at[1], sgu.at[pl.ds(FFP, FF)])
    l_sd = load(sdn_h, sdn.at[pl.ds(0, FF)])
    l_g = load(gu_h.at[0, 0], gu.at[pl.ds(0, FF)])
    l_u = load(gu_h.at[0, 1], gu.at[pl.ds(FFP, FF)])
    l_d = load(dn_h.at[0], dn.at[pl.ds(0, FF)])

    peers = [sibling]
    peers += [dev(yy=at_y(k)) for k in (1, 2, 3)]
    peers += [dev(yy=at_y(k), cc=sc) for k in (1, 2, 3)]
    peers += [dev(xx=at_x(k)) for k in (1, 2, 3)]
    peers += [dev(zz=at_z(k)) for k in range(1, NZ)]
    peers += [dev(zz=at_z(k), yy=at_y(j)) for k in (1, NZ - 1) for j in (1, NY - 1)]
    barrier = pltpu.get_barrier_semaphore()
    for peer in peers:
        pl.semaphore_signal(barrier, inc=1, device_id=peer, device_id_type=MESH)

    zpad = jnp.zeros((FFP - FF, gu.shape[1]), BF16)
    for ref in (gu, sgu):
        ref[FF:FFP, :] = zpad
        ref[FFP + FF : 2 * FFP, :] = zpad
    for ref in (dn, sdn):
        ref[FF:FFP, :] = zpad

    l_attn.wait()
    l_proj.wait()
    for rel in (2, 1, 3, 0):
        d2d_s[rel] = dot_nn(attn[...], proj[:, pl.ds(col(rel, sc), W)]).astype(BF16)
    pl.semaphore_wait(barrier, len(peers))
    c_d2d = {rel: send(d2d_s.at[rel], d2d_r.at[rel], sibling) for rel in (2, 1, 3, 0)}
    c_yr = {}
    for rel in (2, 1, 3):
        part = dot_nn(attn[...], proj[:, pl.ds(col(rel, c), W)])
        c_d2d[rel].wait_recv()
        ys[rel - 1] = (part + d2d_r[rel].astype(F32)).astype(BF16)
        c_yr[rel] = send(ys.at[rel - 1], yr.at[rel - 1], dev(yy=at_y(rel)))
    part = dot_nn(attn[...], proj[:, pl.ds(col(0, c), W)])
    c_d2d[0].wait_recv()
    l_resid.wait()
    own_acc[...] = part + d2d_r[0].astype(F32) + resid[...].astype(F32)

    l_routes.wait()
    experts = NX * NZ * 2
    row = lax.broadcasted_iota(jnp.int32, (experts, T), 0)
    alive = lax.broadcasted_iota(jnp.int32, (experts, T), 1) < live_ref[0]
    wanted = 2 * ((row & 3) * NZ + (row >> 3)) + ((row >> 2) & 1)
    chosen = row == routes[0:1, :]
    named = wanted == routes[0:1, :]
    for k in range(1, routes.shape[0]):
        chosen = chosen | (row == routes[k : k + 1, :])
        named = named | (wanted == routes[k : k + 1, :])
    act_t = jnp.where(named & alive, 1.0, 0.0)
    before = jnp.where(
        lax.broadcasted_iota(jnp.int32, (T, T), 0) < lax.broadcasted_iota(jnp.int32, (T, T), 1), 1.0, 0.0
    ).astype(BF16)
    position = dot_nn(act_t.astype(BF16), before)
    code[...] = jnp.where(act_t > 0.5, position, -1.0)
    s_code = group()
    for k in range(1, NZ):
        send(code.at[pl.ds(pl.multiple_of(at_z(k) * 8, 8), 8)], cz.at[k], dev(zz=at_z(k)), s_code)
    cz[0] = code[pl.ds(pl.multiple_of(z * 8, 8), 8), :]

    for rel in (1, 3, 2):
        c_yr[rel].wait_recv()
    total = own_acc[...]
    for k in range(3):
        total = total + yr[k].astype(F32)
    st[0] = total.astype(BF16)
    ones = jnp.ones((8, W), F32)

    def squares(v):
        return lax.dot_general(
            ones, v * v, (((1,), (1,)), ((), ())), precision=lax.Precision.HIGHEST, preferred_element_type=F32
        )

    def share(src, dst):
        sem = group()
        for k in (2, 1, 3):
            send(src, dst.at[k], dev(yy=at_y(k)), sem)
            send(src, dst.at[3 + k], dev(yy=at_y(k), cc=sc), sem)
        send(src, dst.at[0], sibling, sem)
        return sem

    def inverse(sem, src, dst):
        arrived(sem, dst)
        tot = src[...]
        for k in range(7):
            tot = tot + dst[k]
        return jnp.transpose(lax.rsqrt(tot / (8 * W) + EPS))[:, 0:1]

    ss_s[...] = squares(st[0].astype(F32))
    c_ss = share(ss_s, ss_r)
    c_st = {rel: send(st.at[0], st.at[rel], dev(yy=at_y(NY - rel))) for rel in (1, 3, 2)}
    l_gain.wait()
    l_ngain.wait()
    gain[...] = gain1[...].reshape(8, W)
    ngain[...] = ngain1[...].reshape(8, W)
    slot1 = lax.broadcasted_iota(jnp.int32, (CAP_PAD, T), 0).astype(F32)
    for xp in range(NX):
        own_code = cz[0, pl.ds(grp * 4 + xp, 1), :]
        pmat1[0, xp * CAP_PAD : (xp + 1) * CAP_PAD, :] = jnp.where(slot1 == own_code, 1.0, 0.0).astype(BF16)
    inv = inverse(c_ss, ss_s, ss_r)

    def gain_row(ref, rel):
        return ref[pl.ds(at_y(rel) * 2 + c, 1), :]

    z_right, z_left = dev(zz=at_z(1)), dev(zz=at_z(NZ - 1))
    y_up, y_down = dev(yy=at_y(1)), dev(yy=at_y(NY - 1))
    ring = {}
    yfw = {}

    def normalise(rel):
        if rel > 0:
            c_st[rel].wait_recv()
        nb[0, rel] = (st[rel].astype(F32) * inv * gain_row(gain, rel)).astype(BF16)
        if rel < 2:
            ring["R", 0, rel] = send(nb.at[0, rel], nb.at[1, rel], z_right)
            ring["L", 0, rel] = send(nb.at[0, rel], nb.at[NZ - 1, rel], z_left)

    normalise(0)
    normalise(1)

    s_yfw = {p: group() for p in (1, 2, 3, 4)}

    def ring_step(s):
        for ch in (0, 1):
            for way, got, nxt in (("R", s + 1, s + 2), ("L", NZ - 1 - s, NZ - 2 - s)):
                if s == 3 and ch != (0 if way == "R" else 1):
                    continue
                ring[way, s, ch].wait_recv()
                if s < 2 or (s == 2 and ch == (0 if way == "R" else 1)):
                    ring[way, s + 1, ch] = send(
                        nb.at[got, ch], nb.at[nxt, ch], z_right if way == "R" else z_left
                    )
                if ch == 0:
                    send(nb.at[got, 0], nb.at[got, 3], y_up, s_yfw[s + 1])
                else:
                    send(nb.at[got, 1], nb.at[got, 2], y_down, s_yfw[s + 1])

    slot2 = lax.broadcasted_iota(jnp.int32, (CAP, T), 0).astype(F32)
    slot1 = lax.broadcasted_iota(jnp.int32, (CAP_PAD, T), 0).astype(F32)
    none = jnp.zeros((CAP, T), F32)

    def code_row(ref, k, xp):
        return ref[k, pl.ds(grp * 4 + xp, 1), :]

    def build_slots(p):
        pm = chunk(pmat2, pmat1, p)
        R = per_owner(p)
        for xp in range(NX):
            if len(BLOCKS[p]) == 2:
                a, b = BLOCKS[p]
                pa = jnp.where(slot2 == code_row(cz, a, xp), 1.0, 0.0)
                pb_ = jnp.where(slot2 == code_row(cz, b, xp), 1.0, 0.0)
                block = jnp.concatenate(
                    [jnp.concatenate([pa, none], axis=1), jnp.concatenate([none, pb_], axis=1)], axis=0
                )
            else:
                block = jnp.where(slot1 == code_row(cz, BLOCKS[p][0], xp), 1.0, 0.0)
            pm[xp * R : (xp + 1) * R, :] = block.astype(BF16)

    def build_weights(p):
        pm, wm = chunk(pmat2, pmat1, p), chunk(wmat2, wmat1, p)
        R = per_owner(p)
        parts = []
        for xp in range(NX):
            g = jnp.concatenate([code_row(gz, k, xp) for k in BLOCKS[p]], axis=1)
            parts.append(pm[xp * R : (xp + 1) * R, :].astype(F32) * g)
        wm[...] = jnp.transpose(jnp.concatenate(parts, axis=0)).astype(BF16)

    s_x = {p: group() for p in range(5)}
    l_x = {}

    def owner_rows(k, p):
        R = per_owner(p)
        return pl.ds(pl.multiple_of(at_x(k) * R, 16), R)

    def slots(p, half):
        pm, xs, rows = chunk(pmat2, pmat1, p), chunk(xs2, xs1, p), chunk(rows2, rows1, p)
        for rel in (2 * half, 2 * half + 1):
            picked = None
            for i, k in enumerate(BLOCKS[p]):
                t = dot_nn(pm[:, i * T : (i + 1) * T], nb[k, rel])
                picked = t if picked is None else picked + t
            xs[:, rel * W : (rel + 1) * W] = picked.astype(BF16)
        cols = pl.ds(2 * half * W, 2 * W)
        for k in (2, 1, 3):
            send(xs.at[owner_rows(k, p), cols], rows.at[owner_rows(0, p), cols], dev(xx=at_x(k)), s_x[p])
        if half == 1:
            l_x[p] = local(xs.at[owner_rows(0, p)], rows.at[owner_rows(0, p)])

    c_fw = {}

    def forward(p):
        rows = chunk(rows2, rows1, p)
        l_x[p].wait()
        arrived(s_x[p], rows.at[pl.ds(0, 3 * per_owner(p))])
        c_fw[p] = send(rows, chunk(rsib2, rsib1, p), sibling)

    def swiglu(m, own, sib, weights):
        def up(n, carry):
            units = pl.ds(pl.multiple_of(n * 256, 256), 256)
            acc = None
            for rel in range(4):
                t = dot_nt(own(rel), weights[units, pl.ds(col(rel, c), W)])
                acc = t if acc is None else acc + t
            for rel in range(4):
                acc = acc + dot_nt(sib(rel), weights[units, pl.ds(col(rel, sc), W)])
            gbuf[0:m, units] = acc
            return carry

        lax.fori_loop(0, 2 * FFP // 256, up, 0)

        def act(i, carry):
            part = pl.ds(pl.multiple_of(i * (m // 4), 16), m // 4)
            gate = gbuf[part, 0:FFP]
            hbuf[part, :] = (gate / (1.0 + jnp.exp(-gate)) * gbuf[part, FFP : 2 * FFP]).astype(BF16)
            return carry

        lax.fori_loop(0, 4, act, 0)

    c_t = {}

    def expert(p):
        rows, rsib = chunk(rows2, rows1, p), chunk(rsib2, rsib1, p)
        tsnd, town = chunk(tsnd2, tsnd1, p), chunk(town2, town1, p)
        m = NX * per_owner(p)
        c_fw[p].wait_recv()
        swiglu(
            m,
            lambda rel: rows[:, rel * W : (rel + 1) * W],
            lambda rel: rsib[:, rel * W : (rel + 1) * W],
            gu,
        )
        for rel in range(4):
            t = dot_nn(hbuf[0:m, :], dn[:, pl.ds(col(rel, sc), W)])
            tsnd[:, rel * W : (rel + 1) * W] = t.astype(BF16)
        c_t[p] = send(tsnd, chunk(trcv2, trcv1, p), sibling)
        for rel in range(4):
            t = dot_nn(hbuf[0:m, :], dn[:, pl.ds(col(rel, c), W)])
            town[:, rel * W : (rel + 1) * W] = t.astype(BF16)

    s_ret = {}
    l_ret = {}

    def give_back(p, halves=(1, 0)):
        town, rt = chunk(town2, town1, p), chunk(rt2, rt1, p)
        trcv = chunk(trcv2, trcv1, p)
        if 1 in halves:
            c_t[p].wait_recv()
        for half in halves:
            cols = slice(2 * half * W, 2 * (half + 1) * W)
            window = pl.ds(2 * half * W, 2 * W)
            town[:, cols] = (town[:, cols].astype(F32) + trcv[:, cols].astype(F32)).astype(BF16)
            s_ret[p, half] = group()
            for k in (2, 1, 3):
                send(
                    town.at[owner_rows(k, p), window], rt.at[owner_rows(0, p), window],
                    dev(xx=at_x(k)), s_ret[p, half],
                )
            l_ret[p, half] = local(town.at[owner_rows(0, p), window], rt.at[owner_rows(0, p), window])

    c_y = {}

    def combine(p, halves=(1, 0)):
        wm, rt = chunk(wmat2, wmat1, p), chunk(rt2, rt1, p)
        for rel in (2, 3, 1, 0):
            if rel // 2 not in halves:
                continue
            if rel in (1, 2):
                half = rel // 2
                l_ret[p, half].wait()
                arrived(s_ret[p, half], rt.at[pl.ds(0, 3 * per_owner(p)), pl.ds(2 * half * W, 2 * W)])
            order = list(enumerate(BLOCKS[p]))
            for i, k in order if rel in (2, 1) else order[::-1]:
                got = dot_nn(wm[i * T : (i + 1) * T, :], rt[:, rel * W : (rel + 1) * W])
                if k == 0:
                    got = got + sh_own[rel] + sh_r[rel].astype(F32)
                if rel < 2:
                    pb[k, rel] = got
                elif rel == 2:
                    ysnd[k, 0] = got.astype(BF16)
                    c_y[k, 1] = send(ysnd.at[k, 0], yrcv.at[k, 1], y_up)
                else:
                    ysnd[k, 1] = got.astype(BF16)
                    c_y[k, 0] = send(ysnd.at[k, 1], yrcv.at[k, 0], y_down)

    def wait_y(p):
        k = BLOCKS[p][0]
        arrived(s_yfw[p], nb.at[k] if p < 4 else nb.at[k, pl.ds(0, 2)])

    slots(0, 0)
    for rel in (3, 2):
        normalise(rel)
    c_sib = send(nb.at[0], nsib, sibling)
    slots(0, 1)
    arrived(s_code, cz.at[pl.ds(1, NZ - 1)])
    for p in (1, 2, 3, 4):
        build_slots(p)
    l_router.wait()
    c_sib.wait_recv()
    logits = None
    for rel in range(4):
        t = dot_nt(router[:, pl.ds(col(rel, c), W)], nb[0, rel])
        t = t + dot_nt(router[:, pl.ds(col(rel, sc), W)], nsib[rel])
        logits = t if logits is None else logits + t
    scores = jnp.where(chosen, 1.0 / (1.0 + jnp.exp(-logits)), 0.0)
    gates = scores / jnp.sum(scores, axis=0, keepdims=True) * SCALE
    gates = jnp.where(alive, gates, 0.0).astype(BF16)
    sel_r = lax.broadcasted_iota(jnp.int32, (experts, experts), 0)
    sel_c = lax.broadcasted_iota(jnp.int32, (experts, experts), 1)
    sel_w = 2 * ((sel_r & 3) * NZ + (sel_r >> 3)) + ((sel_r >> 2) & 1)
    gt[...] = dot_nn(jnp.where(sel_c == sel_w, 1.0, 0.0).astype(BF16), gates)
    s_gate = group()
    for k in range(1, NZ):
        send(gt.at[pl.ds(pl.multiple_of(at_z(k) * 8, 8), 8)], gz.at[k], dev(zz=at_z(k)), s_gate)
    gz[0] = gt[pl.ds(pl.multiple_of(z * 8, 8), 8), :]

    ring_step(0)
    slots(1, 0)
    forward(0)
    l_sg.wait()
    l_su.wait()
    l_sd.wait()
    swiglu(T, lambda rel: nb[0, rel], lambda rel: nsib[rel], sgu)
    wait_y(1)
    slots(1, 1)
    ring_step(1)
    slots(2, 0)
    for rel in range(4):
        sh_s[rel] = dot_nn(hbuf[0:T, :], sdn[:, pl.ds(col(rel, sc), W)]).astype(BF16)
    c_sh = send(sh_s, sh_r, sibling)
    for rel in range(4):
        sh_own[rel] = dot_nn(hbuf[0:T, :], sdn[:, pl.ds(col(rel, c), W)])
    l_g.wait()
    l_u.wait()
    l_d.wait()
    expert(0)
    wait_y(2)
    slots(2, 1)
    ring_step(2)
    slots(3, 0)
    forward(1)
    ring_step(3)
    wait_y(3)
    slots(3, 1)
    expert(1)
    wait_y(4)
    slots(4, 0)
    slots(4, 1)
    give_back(0)
    forward(2)
    arrived(s_gate, gz.at[pl.ds(1, NZ - 1)])
    for p in range(5):
        build_weights(p)
    expert(2)
    give_back(1, (1,))
    forward(3)
    forward(4)
    expert(4)
    expert(3)
    give_back(4)
    give_back(3)
    give_back(2)
    give_back(1, (0,))
    c_sh.wait_recv()
    combine(0)
    combine(1, (1,))

    back = {}

    def value(k, ch):
        c_y[k, ch].wait_recv()
        return pb[k, ch] + yrcv[k, ch].astype(F32)

    def pass_on(wi, way, s, ch, k, to):
        v = value(k, ch)
        if (way, s - 1, ch) in back:
            back[way, s - 1, ch].wait_recv()
            v = v + rs_r[wi, s - 1, ch].astype(F32)
        rs_s[wi, s, ch] = v.astype(BF16)
        back[way, s, ch] = send(rs_s.at[wi, s, ch], rs_r.at[wi, s, ch], to)

    last_left = dev(zz=at_z(NZ - 1), yy=at_y(1))
    last_right = dev(zz=at_z(1), yy=at_y(1))
    combine(4)
    pass_on(0, "L", 0, 0, 4, z_left)
    pass_on(1, "R", 0, 1, 4, z_right)
    for s in (1, 2, 3):
        if s == 2:
            fb_s[...] = value(0, 1).astype(BF16)
            c_fb = send(fb_s, fb_r, y_up)
        combine(4 - s, (1, 0) if s < 3 else (0,))
        for ch in (1, 0):
            pass_on(0, "L", s, ch, 4 - s, last_left if s == 3 and ch == 1 else z_left)
            pass_on(1, "R", s, 1 - ch, 4 + s, last_right if s == 3 and ch == 0 else z_right)

    mine = value(0, 0) + st[0].astype(F32)
    c_fb.wait_recv()
    mine = mine + fb_r[...].astype(F32)
    for wi, way, ch in ((0, "L", 1), (1, "R", 0), (0, "L", 0), (1, "R", 1)):
        back[way, 3, ch].wait_recv()
        mine = mine + rs_r[wi, 3, ch].astype(F32)
    nxt = mine.astype(BF16)
    out_s[...] = nxt
    wide = nxt.astype(F32)
    q_s[...] = squares(wide)
    inv2 = inverse(share(q_s, q_r), q_s, q_r)
    out_n[...] = (wide * inv2 * gain_row(ngain, 0)).astype(BF16)
    for cp in copies[-N_SEND:]:
        cp.wait_send()


N_SEND = 32
N_RECV = 94


def on_device(
    attn_out, out_proj, residual, norm_gain, router, expert_gate_up, expert_down,
    shared_gate_up, shared_down, routes, live_rows, next_gain,
):
    T, W = attn_out.shape
    D = out_proj.shape[1]
    FF = expert_down.shape[1]
    FFP = -(-FF // 128) * 128
    H = D // 2
    R2, R1 = NX * 2 * CAP, NX * CAP_PAD
    fanout = routes.shape[1]
    vm = pltpu.VMEM
    both = [vm((3, R2, H), BF16), vm((2, R1, H), BF16)]
    scratch = [
        vm((T, W), BF16), vm((W, D), BF16), vm((T, W), BF16), vm((D,), F32), vm((8, W), F32), vm((64, D), BF16),
        vm((2 * FFP, D), BF16), vm((FFP, D), BF16), vm((2 * FFP, D), BF16), vm((FFP, D), BF16),
        vm((fanout, T), jnp.int32), vm((D,), F32), vm((8, W), F32),
        vm((4, T, W), BF16), vm((4, T, W), BF16), vm((3, T, W), BF16), vm((3, T, W), BF16),
        vm((4, T, W), BF16), vm((T, W), F32), vm((8, T), F32), vm((7, 8, T), F32),
        vm((64, T), F32), vm((NZ, 8, T), F32), vm((64, T), F32), vm((NZ, 8, T), F32),
        vm((NZ, 4, T, W), BF16), vm((4, T, W), BF16),
        vm((3, R2, 2 * T), BF16), vm((2, R1, T), BF16), vm((3, 2 * T, R2), BF16), vm((2, T, R1), BF16),
        *both, *both, *both,
        vm((R2, 2 * FFP), F32), vm((R2, FFP), BF16),
        *both, *both, *both, *both,
        vm((4, T, W), F32), vm((4, T, W), BF16), vm((4, T, W), BF16),
        vm((NZ, 2, T, W), F32), vm((NZ, 2, T, W), BF16), vm((NZ, 2, T, W), BF16),
        vm((2, 4, 2, T, W), BF16), vm((2, 4, 2, T, W), BF16),
        vm((T, W), BF16), vm((T, W), BF16), vm((8, T), F32), vm((7, 8, T), F32),
        pltpu.SemaphoreType.DMA((13,)), pltpu.SemaphoreType.DMA((15,)),
        pltpu.SemaphoreType.DMA((N_SEND,)), pltpu.SemaphoreType.DMA((N_RECV,)),
    ]
    hbm = pl.BlockSpec(memory_space=pl.ANY)
    return pl.pallas_call(
        kernel,
        out_shape=(jax.ShapeDtypeStruct((T, W), BF16), jax.ShapeDtypeStruct((T, W), BF16)),
        in_specs=[pl.BlockSpec(memory_space=pltpu.SMEM)] + [hbm] * 11,
        out_specs=(pl.BlockSpec(memory_space=pltpu.VMEM), pl.BlockSpec(memory_space=pltpu.VMEM)),
        scratch_shapes=scratch,
        compiler_params=pltpu.CompilerParams(
            collective_id=0, has_side_effects=True, vmem_limit_bytes=67043328
        ),
    )(
        live_rows, attn_out, out_proj, residual, norm_gain, router.T, expert_gate_up,
        expert_down, shared_gate_up, shared_down, routes.T, next_gain,
    )


def solution(mesh):
    in_specs = (
        P("ep", "tp"),
        P("tp", None),
        P("ep", None),
        P(),
        P(),
        P(("ep", "tp"), None, None, None),
        P(("ep", "tp"), None, None),
        P(None, "tp", None),
        P("tp", None),
        P("ep", None),
        P("ep"),
        P(),
    )
    out_specs = (P("ep", "tp"), P("ep", "tp"))
    return jax.shard_map(
        on_device, mesh=mesh, in_specs=in_specs, out_specs=out_specs, check_vma=False
    )
```

```python
import jax
import jax.numpy as jnp
from jax import lax
from jax.experimental import pallas as pl
from jax.experimental.pallas import tpu as pltpu
from jax.sharding import PartitionSpec as P

NX, NZ, NY = 4, 8, 4
CAP = 40
CAP_PAD = 48
BLOCKS = {0: (0,), 1: (1, 7), 2: (2, 6), 3: (3, 5), 4: (4,)}
EPS = 1e-06
SCALE = 2.446
F32 = jnp.float32
BF16 = jnp.bfloat16
MESH = pl.DeviceIdType.MESH


def dot_nn(a, b):
    return lax.dot_general(a, b, (((1,), (0,)), ((), ())), preferred_element_type=F32)


def dot_nt(a, b):
    return lax.dot_general(a, b, (((1,), (1,)), ((), ())), preferred_element_type=F32)


def dot_tn(a, b):
    return lax.dot_general(a, b, (((0,), (0,)), ((), ())), preferred_element_type=F32)


def kernel(
    live_ref, attn_h, proj_h, resid_h, gain_h, router_h, gu_h, dn_h, sgu_h, sdn_h, routes_h, ngain_h,
    out_s, out_n,
    attn, proj, resid, gain1, gain, router, gu, dn, sgu, sdn, routes, ngain1, ngain,
    d2d_s, d2d_r, ys, yr, st, own_acc, ss_s, ss_r,
    code, cz, gt, gz,
    nb, nsib, pmat2, pmat1, wmat2, wmat1, xs2, xs1, rows2, rows1, rsib2, rsib1,
    gbuf, hbuf, tsnd2, tsnd1, trcv2, trcv1, town2, town1, rt2, rt1,
    sh_own, sh_s, sh_r,
    pb, ysnd, yrcv, rs_s, rs_r, fb_s, fb_r, q_s, q_r,
    load_sem, local_sem, send_sem, recv_sem,
):
    ep = lax.axis_index("ep")
    tp = lax.axis_index("tp")
    x, z = ep // NZ, lax.rem(ep, NZ)
    y, c = tp // 2, lax.rem(tp, 2)
    grp = y // 2
    sc = 1 - c
    T = attn.shape[0]
    W = attn.shape[1]
    FFP = gu.shape[0] // 2
    FF = gu_h.shape[2]

    def chunk(double, single, p):
        return double.at[p - 1] if 1 <= p <= 3 else single.at[p // 4]

    def per_owner(p):
        return 2 * CAP if 1 <= p <= 3 else CAP_PAD

    def at_y(k):
        return lax.rem(y + k, NY)

    def at_z(k):
        return lax.rem(z + k, NZ)

    def at_x(k):
        return lax.rem(x + k, NX)

    def dev(xx=None, zz=None, yy=None, cc=None):
        xx = x if xx is None else xx
        zz = z if zz is None else zz
        yy = y if yy is None else yy
        cc = c if cc is None else cc
        return (xx * NZ + zz, yy * 2 + cc)

    sibling = dev(cc=sc)

    def col(rel, core):
        return pl.multiple_of((at_y(rel) * 2 + core) * W, W)

    copies = []
    fresh = iter(range(N_RECV))

    def group():
        return next(fresh)

    def send(src, dst, to, sem=None):
        i = len(copies)
        if i >= N_SEND:
            copies[i - N_SEND].wait_send()
        cp = pltpu.make_async_remote_copy(
            src_ref=src, dst_ref=dst, send_sem=send_sem.at[i % N_SEND],
            recv_sem=recv_sem.at[group() if sem is None else sem], device_id=to, device_id_type=MESH,
        )
        cp.start()
        copies.append(cp)
        return cp

    def arrived(sem, size):
        pltpu.make_async_remote_copy(
            src_ref=size, dst_ref=size, send_sem=send_sem.at[0], recv_sem=recv_sem.at[sem],
            device_id=sibling, device_id_type=MESH,
        ).wait_recv()

    loads = []

    def load(src, dst):
        i = len(loads)
        cp = pltpu.make_async_copy(src, dst, load_sem.at[i])
        cp.start()
        loads.append(cp)
        return cp

    locals_ = []

    def local(src, dst):
        i = len(locals_)
        cp = pltpu.make_async_copy(src, dst, local_sem.at[i])
        cp.start()
        locals_.append(cp)
        return cp

    l_attn = load(attn_h, attn)
    l_proj = load(proj_h, proj)
    l_routes = load(routes_h, routes)
    l_resid = load(resid_h.at[:, pl.ds(col(0, c), W)], resid)
    l_gain = load(gain_h, gain1)
    l_ngain = load(ngain_h, ngain1)
    l_router = load(router_h, router)
    l_sg = load(sgu_h.at[0], sgu.at[pl.ds(0, FF)])
    l_su = load(sgu_h.at[1], sgu.at[pl.ds(FFP, FF)])
    l_sd = load(sdn_h, sdn.at[pl.ds(0, FF)])
    l_g = load(gu_h.at[0, 0], gu.at[pl.ds(0, FF)])
    l_u = load(gu_h.at[0, 1], gu.at[pl.ds(FFP, FF)])
    l_d = load(dn_h.at[0], dn.at[pl.ds(0, FF)])

    peers = [sibling]
    peers += [dev(yy=at_y(k)) for k in (1, 2, 3)]
    peers += [dev(yy=at_y(k), cc=sc) for k in (1, 2, 3)]
    peers += [dev(xx=at_x(k)) for k in (1, 2, 3)]
    peers += [dev(zz=at_z(k)) for k in range(1, NZ)]
    barrier = pltpu.get_barrier_semaphore()
    for peer in peers:
        pl.semaphore_signal(barrier, inc=1, device_id=peer, device_id_type=MESH)

    zpad = jnp.zeros((FFP - FF, gu.shape[1]), BF16)
    for ref in (gu, sgu):
        ref[FF:FFP, :] = zpad
        ref[FFP + FF : 2 * FFP, :] = zpad
    for ref in (dn, sdn):
        ref[FF:FFP, :] = zpad

    l_attn.wait()
    l_proj.wait()
    for rel in (2, 1, 3, 0):
        d2d_s[rel] = dot_nn(attn[...], proj[:, pl.ds(col(rel, sc), W)]).astype(BF16)
    pl.semaphore_wait(barrier, len(peers))
    c_d2d = {rel: send(d2d_s.at[rel], d2d_r.at[rel], sibling) for rel in (2, 1, 3, 0)}
    c_yr = {}
    for rel in (2, 1, 3):
        part = dot_nn(attn[...], proj[:, pl.ds(col(rel, c), W)])
        c_d2d[rel].wait_recv()
        ys[rel - 1] = (part + d2d_r[rel].astype(F32)).astype(BF16)
        c_yr[rel] = send(ys.at[rel - 1], yr.at[rel - 1], dev(yy=at_y(rel)))
    part = dot_nn(attn[...], proj[:, pl.ds(col(0, c), W)])
    c_d2d[0].wait_recv()
    l_resid.wait()
    own_acc[...] = part + d2d_r[0].astype(F32) + resid[...].astype(F32)

    l_routes.wait()
    experts = NX * NZ * 2
    row = lax.broadcasted_iota(jnp.int32, (experts, T), 0)
    alive = lax.broadcasted_iota(jnp.int32, (experts, T), 1) < live_ref[0]
    wanted = 2 * ((row & 3) * NZ + (row >> 3)) + ((row >> 2) & 1)
    chosen = row == routes[0:1, :]
    named = wanted == routes[0:1, :]
    for k in range(1, routes.shape[0]):
        chosen = chosen | (row == routes[k : k + 1, :])
        named = named | (wanted == routes[k : k + 1, :])
    act_t = jnp.where(named & alive, 1.0, 0.0)
    before = jnp.where(
        lax.broadcasted_iota(jnp.int32, (T, T), 0) < lax.broadcasted_iota(jnp.int32, (T, T), 1), 1.0, 0.0
    ).astype(BF16)
    position = dot_nn(act_t.astype(BF16), before)
    code[...] = jnp.where(act_t > 0.5, position, -1.0)
    s_code = group()
    for k in range(1, NZ):
        send(code.at[pl.ds(pl.multiple_of(at_z(k) * 8, 8), 8)], cz.at[k], dev(zz=at_z(k)), s_code)
    cz[0] = code[pl.ds(pl.multiple_of(z * 8, 8), 8), :]

    for rel in (1, 3, 2):
        c_yr[rel].wait_recv()
    total = own_acc[...]
    for k in range(3):
        total = total + yr[k].astype(F32)
    st[0] = total.astype(BF16)
    ones = jnp.ones((8, W), F32)

    def squares(v):
        return lax.dot_general(
            ones, v * v, (((1,), (1,)), ((), ())), precision=lax.Precision.HIGHEST, preferred_element_type=F32
        )

    def share(src, dst):
        sem = group()
        for k in (2, 1, 3):
            send(src, dst.at[k], dev(yy=at_y(k)), sem)
            send(src, dst.at[3 + k], dev(yy=at_y(k), cc=sc), sem)
        send(src, dst.at[0], sibling, sem)
        return sem

    def inverse(sem, src, dst):
        arrived(sem, dst)
        tot = src[...]
        for k in range(7):
            tot = tot + dst[k]
        return jnp.transpose(lax.rsqrt(tot / (8 * W) + EPS))[:, 0:1]

    ss_s[...] = squares(st[0].astype(F32))
    c_ss = share(ss_s, ss_r)
    c_st = {rel: send(st.at[0], st.at[rel], dev(yy=at_y(NY - rel))) for rel in (1, 3, 2)}
    l_gain.wait()
    l_ngain.wait()
    gain[...] = gain1[...].reshape(8, W)
    ngain[...] = ngain1[...].reshape(8, W)
    slot1 = lax.broadcasted_iota(jnp.int32, (CAP_PAD, T), 0).astype(F32)
    for xp in range(NX):
        own_code = cz[0, pl.ds(grp * 4 + xp, 1), :]
        pmat1[0, xp * CAP_PAD : (xp + 1) * CAP_PAD, :] = jnp.where(slot1 == own_code, 1.0, 0.0).astype(BF16)
    inv = inverse(c_ss, ss_s, ss_r)

    def gain_row(ref, rel):
        return ref[pl.ds(at_y(rel) * 2 + c, 1), :]

    z_right, z_left = dev(zz=at_z(1)), dev(zz=at_z(NZ - 1))
    y_up, y_down = dev(yy=at_y(1)), dev(yy=at_y(NY - 1))
    ring = {}
    yfw = {}

    def normalise(rel):
        if rel > 0:
            c_st[rel].wait_recv()
        nb[0, rel] = (st[rel].astype(F32) * inv * gain_row(gain, rel)).astype(BF16)
        if rel < 2:
            ring["R", 0, rel] = send(nb.at[0, rel], nb.at[1, rel], z_right)
            ring["L", 0, rel] = send(nb.at[0, rel], nb.at[NZ - 1, rel], z_left)

    normalise(0)
    normalise(1)

    s_yfw = {p: group() for p in (1, 2, 3, 4)}

    def ring_step(s):
        for ch in (0, 1):
            for way, got, nxt in (("R", s + 1, s + 2), ("L", NZ - 1 - s, NZ - 2 - s)):
                if s == 3 and ch != (0 if way == "R" else 1):
                    continue
                ring[way, s, ch].wait_recv()
                if s < 2 or (s == 2 and ch == (0 if way == "R" else 1)):
                    ring[way, s + 1, ch] = send(
                        nb.at[got, ch], nb.at[nxt, ch], z_right if way == "R" else z_left
                    )
                if ch == 0:
                    send(nb.at[got, 0], nb.at[got, 3], y_up, s_yfw[s + 1])
                else:
                    send(nb.at[got, 1], nb.at[got, 2], y_down, s_yfw[s + 1])

    slot2 = lax.broadcasted_iota(jnp.int32, (CAP, T), 0).astype(F32)
    slot1 = lax.broadcasted_iota(jnp.int32, (CAP_PAD, T), 0).astype(F32)
    none = jnp.zeros((CAP, T), F32)

    def code_row(ref, k, xp):
        return ref[k, pl.ds(grp * 4 + xp, 1), :]

    def build_slots(p):
        pm = chunk(pmat2, pmat1, p)
        R = per_owner(p)
        for xp in range(NX):
            if len(BLOCKS[p]) == 2:
                a, b = BLOCKS[p]
                pa = jnp.where(slot2 == code_row(cz, a, xp), 1.0, 0.0)
                pb_ = jnp.where(slot2 == code_row(cz, b, xp), 1.0, 0.0)
                block = jnp.concatenate(
                    [jnp.concatenate([pa, none], axis=1), jnp.concatenate([none, pb_], axis=1)], axis=0
                )
            else:
                block = jnp.where(slot1 == code_row(cz, BLOCKS[p][0], xp), 1.0, 0.0)
            pm[xp * R : (xp + 1) * R, :] = block.astype(BF16)

    def build_weights(p):
        pm, wm = chunk(pmat2, pmat1, p), chunk(wmat2, wmat1, p)
        R = per_owner(p)
        parts = []
        for xp in range(NX):
            g = jnp.concatenate([code_row(gz, k, xp) for k in BLOCKS[p]], axis=1)
            parts.append(pm[xp * R : (xp + 1) * R, :].astype(F32) * g)
        wm[...] = jnp.transpose(jnp.concatenate(parts, axis=0)).astype(BF16)

    s_x = {p: group() for p in range(5)}
    l_x = {}

    def owner_rows(k, p):
        R = per_owner(p)
        return pl.ds(pl.multiple_of(at_x(k) * R, 16), R)

    def slots(p, half):
        pm, xs, rows = chunk(pmat2, pmat1, p), chunk(xs2, xs1, p), chunk(rows2, rows1, p)
        for rel in (2 * half, 2 * half + 1):
            picked = None
            for i, k in enumerate(BLOCKS[p]):
                t = dot_nn(pm[:, i * T : (i + 1) * T], nb[k, rel])
                picked = t if picked is None else picked + t
            xs[:, rel * W : (rel + 1) * W] = picked.astype(BF16)
        cols = pl.ds(2 * half * W, 2 * W)
        for k in (2, 1, 3):
            send(xs.at[owner_rows(k, p), cols], rows.at[owner_rows(0, p), cols], dev(xx=at_x(k)), s_x[p])
        if half == 1:
            l_x[p] = local(xs.at[owner_rows(0, p)], rows.at[owner_rows(0, p)])

    c_fw = {}

    def forward(p):
        rows = chunk(rows2, rows1, p)
        l_x[p].wait()
        arrived(s_x[p], rows.at[pl.ds(0, 3 * per_owner(p))])
        c_fw[p] = send(rows, chunk(rsib2, rsib1, p), sibling)

    def swiglu(m, own, sib, weights):
        def up(n, carry):
            units = pl.ds(pl.multiple_of(n * 256, 256), 256)
            acc = None
            for rel in range(4):
                t = dot_nt(own(rel), weights[units, pl.ds(col(rel, c), W)])
                acc = t if acc is None else acc + t
            for rel in range(4):
                acc = acc + dot_nt(sib(rel), weights[units, pl.ds(col(rel, sc), W)])
            gbuf[0:m, units] = acc
            return carry

        lax.fori_loop(0, 2 * FFP // 256, up, 0)

        def act(i, carry):
            part = pl.ds(pl.multiple_of(i * (m // 4), 16), m // 4)
            gate = gbuf[part, 0:FFP]
            hbuf[part, :] = (gate / (1.0 + jnp.exp(-gate)) * gbuf[part, FFP : 2 * FFP]).astype(BF16)
            return carry

        lax.fori_loop(0, 4, act, 0)

    c_t = {}

    def expert(p):
        rows, rsib = chunk(rows2, rows1, p), chunk(rsib2, rsib1, p)
        tsnd, town = chunk(tsnd2, tsnd1, p), chunk(town2, town1, p)
        m = NX * per_owner(p)
        c_fw[p].wait_recv()
        swiglu(
            m,
            lambda rel: rows[:, rel * W : (rel + 1) * W],
            lambda rel: rsib[:, rel * W : (rel + 1) * W],
            gu,
        )
        for rel in range(4):
            t = dot_nn(hbuf[0:m, :], dn[:, pl.ds(col(rel, sc), W)])
            tsnd[:, rel * W : (rel + 1) * W] = t.astype(BF16)
        c_t[p] = send(tsnd, chunk(trcv2, trcv1, p), sibling)
        for rel in range(4):
            t = dot_nn(hbuf[0:m, :], dn[:, pl.ds(col(rel, c), W)])
            town[:, rel * W : (rel + 1) * W] = t.astype(BF16)

    s_ret = {}
    l_ret = {}

    def give_back(p):
        town, rt = chunk(town2, town1, p), chunk(rt2, rt1, p)
        trcv = chunk(trcv2, trcv1, p)
        c_t[p].wait_recv()
        for half in (1, 0):
            cols = slice(2 * half * W, 2 * (half + 1) * W)
            window = pl.ds(2 * half * W, 2 * W)
            town[:, cols] = (town[:, cols].astype(F32) + trcv[:, cols].astype(F32)).astype(BF16)
            s_ret[p, half] = group()
            for k in (2, 1, 3):
                send(
                    town.at[owner_rows(k, p), window], rt.at[owner_rows(0, p), window],
                    dev(xx=at_x(k)), s_ret[p, half],
                )
        l_ret[p] = local(town.at[owner_rows(0, p)], rt.at[owner_rows(0, p)])

    c_y = {}

    def combine(p):
        wm, rt = chunk(wmat2, wmat1, p), chunk(rt2, rt1, p)
        l_ret[p].wait()
        for rel in (2, 3, 1, 0):
            if rel in (1, 2):
                half = rel // 2
                arrived(s_ret[p, half], rt.at[pl.ds(0, 3 * per_owner(p)), pl.ds(2 * half * W, 2 * W)])
            order = list(enumerate(BLOCKS[p]))
            for i, k in order if rel in (2, 1) else order[::-1]:
                got = dot_nn(wm[i * T : (i + 1) * T, :], rt[:, rel * W : (rel + 1) * W])
                if k == 0:
                    got = got + sh_own[rel] + sh_r[rel].astype(F32)
                if rel < 2:
                    pb[k, rel] = got
                elif rel == 2:
                    ysnd[k, 0] = got.astype(BF16)
                    c_y[k, 1] = send(ysnd.at[k, 0], yrcv.at[k, 1], y_up)
                else:
                    ysnd[k, 1] = got.astype(BF16)
                    c_y[k, 0] = send(ysnd.at[k, 1], yrcv.at[k, 0], y_down)

    def wait_y(p):
        k = BLOCKS[p][0]
        arrived(s_yfw[p], nb.at[k] if p < 4 else nb.at[k, pl.ds(0, 2)])

    slots(0, 0)
    for rel in (3, 2):
        normalise(rel)
    c_sib = send(nb.at[0], nsib, sibling)
    slots(0, 1)
    arrived(s_code, cz.at[pl.ds(1, NZ - 1)])
    for p in (1, 2, 3, 4):
        build_slots(p)
    l_router.wait()
    c_sib.wait_recv()
    logits = None
    for rel in range(4):
        t = dot_nt(router[:, pl.ds(col(rel, c), W)], nb[0, rel])
        t = t + dot_nt(router[:, pl.ds(col(rel, sc), W)], nsib[rel])
        logits = t if logits is None else logits + t
    scores = jnp.where(chosen, 1.0 / (1.0 + jnp.exp(-logits)), 0.0)
    gates = scores / jnp.sum(scores, axis=0, keepdims=True) * SCALE
    gates = jnp.where(alive, gates, 0.0).astype(BF16)
    sel_r = lax.broadcasted_iota(jnp.int32, (experts, experts), 0)
    sel_c = lax.broadcasted_iota(jnp.int32, (experts, experts), 1)
    sel_w = 2 * ((sel_r & 3) * NZ + (sel_r >> 3)) + ((sel_r >> 2) & 1)
    gt[...] = dot_nn(jnp.where(sel_c == sel_w, 1.0, 0.0).astype(BF16), gates)
    s_gate = group()
    for k in range(1, NZ):
        send(gt.at[pl.ds(pl.multiple_of(at_z(k) * 8, 8), 8)], gz.at[k], dev(zz=at_z(k)), s_gate)
    gz[0] = gt[pl.ds(pl.multiple_of(z * 8, 8), 8), :]

    ring_step(0)
    slots(1, 0)
    forward(0)
    l_sg.wait()
    l_su.wait()
    l_sd.wait()
    swiglu(T, lambda rel: nb[0, rel], lambda rel: nsib[rel], sgu)
    wait_y(1)
    slots(1, 1)
    ring_step(1)
    slots(2, 0)
    for rel in range(4):
        sh_s[rel] = dot_nn(hbuf[0:T, :], sdn[:, pl.ds(col(rel, sc), W)]).astype(BF16)
    c_sh = send(sh_s, sh_r, sibling)
    for rel in range(4):
        sh_own[rel] = dot_nn(hbuf[0:T, :], sdn[:, pl.ds(col(rel, c), W)])
    l_g.wait()
    l_u.wait()
    l_d.wait()
    expert(0)
    wait_y(2)
    slots(2, 1)
    ring_step(2)
    slots(3, 0)
    forward(1)
    ring_step(3)
    wait_y(3)
    slots(3, 1)
    wait_y(4)
    slots(4, 0)
    slots(4, 1)
    give_back(0)
    expert(1)
    forward(2)
    arrived(s_gate, gz.at[pl.ds(1, NZ - 1)])
    for p in range(5):
        build_weights(p)
    expert(2)
    forward(3)
    expert(3)
    forward(4)
    expert(4)
    give_back(4)
    give_back(3)
    give_back(2)
    give_back(1)
    c_sh.wait_recv()
    combine(0)

    back = {}

    def value(k, ch):
        c_y[k, ch].wait_recv()
        return pb[k, ch] + yrcv[k, ch].astype(F32)

    def pass_on(wi, way, s, ch, k, to):
        v = value(k, ch)
        if (way, s - 1, ch) in back:
            back[way, s - 1, ch].wait_recv()
            v = v + rs_r[wi, s - 1, ch].astype(F32)
        rs_s[wi, s, ch] = v.astype(BF16)
        back[way, s, ch] = send(rs_s.at[wi, s, ch], rs_r.at[wi, s, ch], to)

    combine(4)
    pass_on(0, "L", 0, 0, 4, z_left)
    pass_on(1, "R", 0, 1, 4, z_right)
    for s in (1, 2, 3):
        combine(4 - s)
        for ch in (1, 0):
            pass_on(0, "L", s, ch, 4 - s, z_left)
            pass_on(1, "R", s, 1 - ch, 4 + s, z_right)

    def finish(ch):
        v = value(0, ch)
        for wi, way in ((0, "L"), (1, "R")):
            back[way, 3, ch].wait_recv()
            v = v + rs_r[wi, 3, ch].astype(F32)
        return v

    fb_s[...] = finish(1).astype(BF16)
    c_fb = send(fb_s, fb_r, y_up)
    mine = finish(0) + st[0].astype(F32)
    c_fb.wait_recv()
    nxt = (mine + fb_r[...].astype(F32)).astype(BF16)
    wide = nxt.astype(F32)
    out_s[...] = wide
    q_s[...] = squares(wide)
    inv2 = inverse(share(q_s, q_r), q_s, q_r)
    out_n[...] = inv2 * gain_row(ngain, 0)
    for cp in copies[-N_SEND:]:
        cp.wait_send()


N_SEND = 32
N_RECV = 94


def on_device(
    attn_out, out_proj, residual, norm_gain, router, expert_gate_up, expert_down,
    shared_gate_up, shared_down, routes, live_rows, next_gain,
):
    T, W = attn_out.shape
    D = out_proj.shape[1]
    FF = expert_down.shape[1]
    FFP = -(-FF // 128) * 128
    H = D // 2
    R2, R1 = NX * 2 * CAP, NX * CAP_PAD
    fanout = routes.shape[1]
    vm = pltpu.VMEM
    both = [vm((3, R2, H), BF16), vm((2, R1, H), BF16)]
    scratch = [
        vm((T, W), BF16), vm((W, D), BF16), vm((T, W), BF16), vm((D,), F32), vm((8, W), F32), vm((64, D), BF16),
        vm((2 * FFP, D), BF16), vm((FFP, D), BF16), vm((2 * FFP, D), BF16), vm((FFP, D), BF16),
        vm((fanout, T), jnp.int32), vm((D,), F32), vm((8, W), F32),
        vm((4, T, W), BF16), vm((4, T, W), BF16), vm((3, T, W), BF16), vm((3, T, W), BF16),
        vm((4, T, W), BF16), vm((T, W), F32), vm((8, T), F32), vm((7, 8, T), F32),
        vm((64, T), F32), vm((NZ, 8, T), F32), vm((64, T), F32), vm((NZ, 8, T), F32),
        vm((NZ, 4, T, W), BF16), vm((4, T, W), BF16),
        vm((3, R2, 2 * T), BF16), vm((2, R1, T), BF16), vm((3, 2 * T, R2), BF16), vm((2, T, R1), BF16),
        *both, *both, *both,
        vm((R2, 2 * FFP), F32), vm((R2, FFP), BF16),
        *both, *both, *both, *both,
        vm((4, T, W), F32), vm((4, T, W), BF16), vm((4, T, W), BF16),
        vm((NZ, 2, T, W), F32), vm((NZ, 2, T, W), BF16), vm((NZ, 2, T, W), BF16),
        vm((2, 4, 2, T, W), BF16), vm((2, 4, 2, T, W), BF16),
        vm((T, W), BF16), vm((T, W), BF16), vm((8, T), F32), vm((7, 8, T), F32),
        pltpu.SemaphoreType.DMA((13,)), pltpu.SemaphoreType.DMA((10,)),
        pltpu.SemaphoreType.DMA((N_SEND,)), pltpu.SemaphoreType.DMA((N_RECV,)),
    ]
    hbm = pl.BlockSpec(memory_space=pl.ANY)
    stream, scale = pl.pallas_call(
        kernel,
        out_shape=(jax.ShapeDtypeStruct((T, W), F32), jax.ShapeDtypeStruct((T, W), F32)),
        in_specs=[pl.BlockSpec(memory_space=pltpu.SMEM)] + [hbm] * 11,
        out_specs=(pl.BlockSpec(memory_space=pltpu.VMEM), pl.BlockSpec(memory_space=pltpu.VMEM)),
        scratch_shapes=scratch,
        compiler_params=pltpu.CompilerParams(
            collective_id=0, has_side_effects=True, vmem_limit_bytes=67043328
        ),
    )(
        live_rows, attn_out, out_proj, residual, norm_gain, router.T, expert_gate_up,
        expert_down, shared_gate_up, shared_down, routes.T, next_gain,
    )
    return stream.astype(BF16), (stream * scale).astype(BF16)


def solution(mesh):
    in_specs = (
        P("ep", "tp"),
        P("tp", None),
        P("ep", None),
        P(),
        P(),
        P(("ep", "tp"), None, None, None),
        P(("ep", "tp"), None, None),
        P(None, "tp", None),
        P("tp", None),
        P("ep", None),
        P("ep"),
        P(),
    )
    out_specs = (P("ep", "tp"), P("ep", "tp"))
    return jax.shard_map(
        on_device, mesh=mesh, in_specs=in_specs, out_specs=out_specs, check_vma=False
    )
```

```python
import jax
import jax.numpy as jnp
from jax import lax
from jax.experimental import pallas as pl
from jax.experimental.pallas import tpu as pltpu
from jax.sharding import PartitionSpec as P

NX, NZ, NY = 4, 8, 4
CAP = 40
CAP_PAD = 48
BLOCKS = {0: (0,), 1: (1, 7), 2: (2, 6), 3: (3, 5), 4: (4,)}
EPS = 1e-06
SCALE = 2.446
F32 = jnp.float32
BF16 = jnp.bfloat16
MESH = pl.DeviceIdType.MESH


def dot_nn(a, b):
    return lax.dot_general(a, b, (((1,), (0,)), ((), ())), preferred_element_type=F32)


def dot_nt(a, b):
    return lax.dot_general(a, b, (((1,), (1,)), ((), ())), preferred_element_type=F32)


def dot_tn(a, b):
    return lax.dot_general(a, b, (((0,), (0,)), ((), ())), preferred_element_type=F32)


def kernel(
    live_ref, attn_h, proj_h, resid_h, gain_h, router_h, gu_h, dn_h, sgu_h, sdn_h, routes_h, ngain_h,
    out_s, out_n,
    attn, proj, resid, gain1, gain, router, gu, dn, sgu, sdn, routes, ngain1, ngain,
    d2d_s, d2d_r, ys, yr, st, own_acc, ss_s, ss_r,
    code, cz, gt, gz,
    nb, nsib, pmat2, pmat1, wmat2, wmat1, xs2, xs1, rows2, rows1, rsib2, rsib1,
    gbuf, hbuf, tsnd2, tsnd1, trcv2, trcv1, town2, town1, rt2, rt1,
    sh_own, sh_s, sh_r,
    pb, ysnd, yrcv, rs_s, rs_r, fb_s, fb_r, q_s, q_r,
    load_sem, local_sem, send_sem, recv_sem,
):
    ep = lax.axis_index("ep")
    tp = lax.axis_index("tp")
    x, z = ep // NZ, lax.rem(ep, NZ)
    y, c = tp // 2, lax.rem(tp, 2)
    grp = y // 2
    sc = 1 - c
    T = attn.shape[0]
    W = attn.shape[1]
    FFP = gu.shape[0] // 2
    FF = gu_h.shape[2]

    def chunk(double, single, p):
        return double.at[p - 1] if 1 <= p <= 3 else single.at[p // 4]

    def per_owner(p):
        return 2 * CAP if 1 <= p <= 3 else CAP_PAD

    def at_y(k):
        return lax.rem(y + k, NY)

    def at_z(k):
        return lax.rem(z + k, NZ)

    def at_x(k):
        return lax.rem(x + k, NX)

    def dev(xx=None, zz=None, yy=None, cc=None):
        xx = x if xx is None else xx
        zz = z if zz is None else zz
        yy = y if yy is None else yy
        cc = c if cc is None else cc
        return (xx * NZ + zz, yy * 2 + cc)

    sibling = dev(cc=sc)

    def col(rel, core):
        return pl.multiple_of((at_y(rel) * 2 + core) * W, W)

    copies = []
    fresh = iter(range(N_RECV))

    def group():
        return next(fresh)

    def send(src, dst, to, sem=None):
        i = len(copies)
        if i >= N_SEND:
            copies[i - N_SEND].wait_send()
        cp = pltpu.make_async_remote_copy(
            src_ref=src, dst_ref=dst, send_sem=send_sem.at[i % N_SEND],
            recv_sem=recv_sem.at[group() if sem is None else sem], device_id=to, device_id_type=MESH,
        )
        cp.start()
        copies.append(cp)
        return cp

    def arrived(sem, size):
        pltpu.make_async_remote_copy(
            src_ref=size, dst_ref=size, send_sem=send_sem.at[0], recv_sem=recv_sem.at[sem],
            device_id=sibling, device_id_type=MESH,
        ).wait_recv()

    loads = []

    def load(src, dst):
        i = len(loads)
        cp = pltpu.make_async_copy(src, dst, load_sem.at[i])
        cp.start()
        loads.append(cp)
        return cp

    locals_ = []

    def local(src, dst):
        i = len(locals_)
        cp = pltpu.make_async_copy(src, dst, local_sem.at[i])
        cp.start()
        locals_.append(cp)
        return cp

    l_attn = load(attn_h, attn)
    l_proj = load(proj_h, proj)
    l_routes = load(routes_h, routes)
    l_resid = load(resid_h.at[:, pl.ds(col(0, c), W)], resid)
    l_gain = load(gain_h, gain1)
    l_ngain = load(ngain_h, ngain1)
    l_router = load(router_h, router)
    l_sg = load(sgu_h.at[0], sgu.at[pl.ds(0, FF)])
    l_su = load(sgu_h.at[1], sgu.at[pl.ds(FFP, FF)])
    l_sd = load(sdn_h, sdn.at[pl.ds(0, FF)])
    l_g = load(gu_h.at[0, 0], gu.at[pl.ds(0, FF)])
    l_u = load(gu_h.at[0, 1], gu.at[pl.ds(FFP, FF)])
    l_d = load(dn_h.at[0], dn.at[pl.ds(0, FF)])

    peers = [sibling]
    peers += [dev(yy=at_y(k)) for k in (1, 2, 3)]
    peers += [dev(yy=at_y(k), cc=sc) for k in (1, 2, 3)]
    peers += [dev(xx=at_x(k)) for k in (1, 2, 3)]
    peers += [dev(zz=at_z(k)) for k in range(1, NZ)]
    barrier = pltpu.get_barrier_semaphore()
    for peer in peers:
        pl.semaphore_signal(barrier, inc=1, device_id=peer, device_id_type=MESH)

    zpad = jnp.zeros((FFP - FF, gu.shape[1]), BF16)
    for ref in (gu, sgu):
        ref[FF:FFP, :] = zpad
        ref[FFP + FF : 2 * FFP, :] = zpad
    for ref in (dn, sdn):
        ref[FF:FFP, :] = zpad

    l_attn.wait()
    l_proj.wait()
    for rel in (2, 1, 3, 0):
        d2d_s[rel] = dot_nn(attn[...], proj[:, pl.ds(col(rel, sc), W)]).astype(BF16)
    pl.semaphore_wait(barrier, len(peers))
    c_d2d = {rel: send(d2d_s.at[rel], d2d_r.at[rel], sibling) for rel in (2, 1, 3, 0)}
    c_yr = {}
    for rel in (2, 1, 3):
        part = dot_nn(attn[...], proj[:, pl.ds(col(rel, c), W)])
        c_d2d[rel].wait_recv()
        ys[rel - 1] = (part + d2d_r[rel].astype(F32)).astype(BF16)
        c_yr[rel] = send(ys.at[rel - 1], yr.at[rel - 1], dev(yy=at_y(rel)))
    part = dot_nn(attn[...], proj[:, pl.ds(col(0, c), W)])
    c_d2d[0].wait_recv()
    l_resid.wait()
    own_acc[...] = part + d2d_r[0].astype(F32) + resid[...].astype(F32)

    l_routes.wait()
    experts = NX * NZ * 2
    row = lax.broadcasted_iota(jnp.int32, (experts, T), 0)
    alive = lax.broadcasted_iota(jnp.int32, (experts, T), 1) < live_ref[0]
    wanted = 2 * ((row & 3) * NZ + (row >> 3)) + ((row >> 2) & 1)
    chosen = row == routes[0:1, :]
    named = wanted == routes[0:1, :]
    for k in range(1, routes.shape[0]):
        chosen = chosen | (row == routes[k : k + 1, :])
        named = named | (wanted == routes[k : k + 1, :])
    act_t = jnp.where(named & alive, 1.0, 0.0)
    before = jnp.where(
        lax.broadcasted_iota(jnp.int32, (T, T), 0) < lax.broadcasted_iota(jnp.int32, (T, T), 1), 1.0, 0.0
    ).astype(BF16)
    position = dot_nn(act_t.astype(BF16), before)
    code[...] = jnp.where(act_t > 0.5, position, -1.0)
    s_code = group()
    for k in range(1, NZ):
        send(code.at[pl.ds(pl.multiple_of(at_z(k) * 8, 8), 8)], cz.at[k], dev(zz=at_z(k)), s_code)
    cz[0] = code[pl.ds(pl.multiple_of(z * 8, 8), 8), :]

    for rel in (1, 3, 2):
        c_yr[rel].wait_recv()
    total = own_acc[...]
    for k in range(3):
        total = total + yr[k].astype(F32)
    st[0] = total.astype(BF16)
    ones = jnp.ones((8, W), F32)

    def squares(v):
        return lax.dot_general(
            ones, v * v, (((1,), (1,)), ((), ())), precision=lax.Precision.HIGHEST, preferred_element_type=F32
        )

    def share(src, dst):
        sem = group()
        for k in (2, 1, 3):
            send(src, dst.at[k], dev(yy=at_y(k)), sem)
            send(src, dst.at[3 + k], dev(yy=at_y(k), cc=sc), sem)
        send(src, dst.at[0], sibling, sem)
        return sem

    def inverse(sem, src, dst):
        arrived(sem, dst)
        tot = src[...]
        for k in range(7):
            tot = tot + dst[k]
        return jnp.transpose(lax.rsqrt(tot / (8 * W) + EPS))[:, 0:1]

    ss_s[...] = squares(st[0].astype(F32))
    c_ss = share(ss_s, ss_r)
    c_st = {rel: send(st.at[0], st.at[rel], dev(yy=at_y(NY - rel))) for rel in (1, 3, 2)}
    l_gain.wait()
    l_ngain.wait()
    gain[...] = gain1[...].reshape(8, W)
    ngain[...] = ngain1[...].reshape(8, W)
    slot1 = lax.broadcasted_iota(jnp.int32, (CAP_PAD, T), 0).astype(F32)
    for xp in range(NX):
        own_code = cz[0, pl.ds(grp * 4 + xp, 1), :]
        pmat1[0, xp * CAP_PAD : (xp + 1) * CAP_PAD, :] = jnp.where(slot1 == own_code, 1.0, 0.0).astype(BF16)
    inv = inverse(c_ss, ss_s, ss_r)

    def gain_row(ref, rel):
        return ref[pl.ds(at_y(rel) * 2 + c, 1), :]

    z_right, z_left = dev(zz=at_z(1)), dev(zz=at_z(NZ - 1))
    y_up, y_down = dev(yy=at_y(1)), dev(yy=at_y(NY - 1))
    ring = {}
    yfw = {}

    def normalise(rel):
        if rel > 0:
            c_st[rel].wait_recv()
        nb[0, rel] = (st[rel].astype(F32) * inv * gain_row(gain, rel)).astype(BF16)
        if rel < 2:
            ring["R", 0, rel] = send(nb.at[0, rel], nb.at[1, rel], z_right)
            ring["L", 0, rel] = send(nb.at[0, rel], nb.at[NZ - 1, rel], z_left)

    normalise(0)
    normalise(1)

    s_yfw = {p: group() for p in (1, 2, 3, 4)}

    def ring_step(s):
        for ch in (0, 1):
            for way, got, nxt in (("R", s + 1, s + 2), ("L", NZ - 1 - s, NZ - 2 - s)):
                if s == 3 and ch != (0 if way == "R" else 1):
                    continue
                ring[way, s, ch].wait_recv()
                if s < 2 or (s == 2 and ch == (0 if way == "R" else 1)):
                    ring[way, s + 1, ch] = send(
                        nb.at[got, ch], nb.at[nxt, ch], z_right if way == "R" else z_left
                    )
                if ch == 0:
                    send(nb.at[got, 0], nb.at[got, 3], y_up, s_yfw[s + 1])
                else:
                    send(nb.at[got, 1], nb.at[got, 2], y_down, s_yfw[s + 1])

    slot2 = lax.broadcasted_iota(jnp.int32, (CAP, T), 0).astype(F32)
    slot1 = lax.broadcasted_iota(jnp.int32, (CAP_PAD, T), 0).astype(F32)
    none = jnp.zeros((CAP, T), F32)

    def code_row(ref, k, xp):
        return ref[k, pl.ds(grp * 4 + xp, 1), :]

    def build_slots(p):
        pm = chunk(pmat2, pmat1, p)
        R = per_owner(p)
        for xp in range(NX):
            if len(BLOCKS[p]) == 2:
                a, b = BLOCKS[p]
                pa = jnp.where(slot2 == code_row(cz, a, xp), 1.0, 0.0)
                pb_ = jnp.where(slot2 == code_row(cz, b, xp), 1.0, 0.0)
                block = jnp.concatenate(
                    [jnp.concatenate([pa, none], axis=1), jnp.concatenate([none, pb_], axis=1)], axis=0
                )
            else:
                block = jnp.where(slot1 == code_row(cz, BLOCKS[p][0], xp), 1.0, 0.0)
            pm[xp * R : (xp + 1) * R, :] = block.astype(BF16)

    def build_weights(p):
        pm, wm = chunk(pmat2, pmat1, p), chunk(wmat2, wmat1, p)
        R = per_owner(p)
        parts = []
        for xp in range(NX):
            g = jnp.concatenate([code_row(gz, k, xp) for k in BLOCKS[p]], axis=1)
            parts.append(pm[xp * R : (xp + 1) * R, :].astype(F32) * g)
        wm[...] = jnp.transpose(jnp.concatenate(parts, axis=0)).astype(BF16)

    s_x = {p: group() for p in range(5)}
    l_x = {}

    def owner_rows(k, p):
        R = per_owner(p)
        return pl.ds(pl.multiple_of(at_x(k) * R, 16), R)

    def slots(p, half):
        pm, xs, rows = chunk(pmat2, pmat1, p), chunk(xs2, xs1, p), chunk(rows2, rows1, p)
        for rel in (2 * half, 2 * half + 1):
            picked = None
            for i, k in enumerate(BLOCKS[p]):
                t = dot_nn(pm[:, i * T : (i + 1) * T], nb[k, rel])
                picked = t if picked is None else picked + t
            xs[:, rel * W : (rel + 1) * W] = picked.astype(BF16)
        cols = pl.ds(2 * half * W, 2 * W)
        for k in (2, 1, 3):
            send(xs.at[owner_rows(k, p), cols], rows.at[owner_rows(0, p), cols], dev(xx=at_x(k)), s_x[p])
        if half == 1:
            l_x[p] = local(xs.at[owner_rows(0, p)], rows.at[owner_rows(0, p)])

    c_fw = {}

    def forward(p):
        rows = chunk(rows2, rows1, p)
        l_x[p].wait()
        arrived(s_x[p], rows.at[pl.ds(0, 3 * per_owner(p))])
        c_fw[p] = send(rows, chunk(rsib2, rsib1, p), sibling)

    def swiglu(m, own, sib, weights):
        def up(n, carry):
            units = pl.ds(pl.multiple_of(n * 256, 256), 256)
            acc = None
            for rel in range(4):
                t = dot_nt(own(rel), weights[units, pl.ds(col(rel, c), W)])
                acc = t if acc is None else acc + t
            for rel in range(4):
                acc = acc + dot_nt(sib(rel), weights[units, pl.ds(col(rel, sc), W)])
            gbuf[0:m, units] = acc
            return carry

        lax.fori_loop(0, 2 * FFP // 256, up, 0)

        def act(i, carry):
            part = pl.ds(pl.multiple_of(i * (m // 4), 16), m // 4)
            gate = gbuf[part, 0:FFP]
            hbuf[part, :] = (gate / (1.0 + jnp.exp(-gate)) * gbuf[part, FFP : 2 * FFP]).astype(BF16)
            return carry

        lax.fori_loop(0, 4, act, 0)

    c_t = {}

    def expert(p):
        rows, rsib = chunk(rows2, rows1, p), chunk(rsib2, rsib1, p)
        tsnd, town = chunk(tsnd2, tsnd1, p), chunk(town2, town1, p)
        m = NX * per_owner(p)
        c_fw[p].wait_recv()
        swiglu(
            m,
            lambda rel: rows[:, rel * W : (rel + 1) * W],
            lambda rel: rsib[:, rel * W : (rel + 1) * W],
            gu,
        )
        for rel in range(4):
            t = dot_nn(hbuf[0:m, :], dn[:, pl.ds(col(rel, sc), W)])
            tsnd[:, rel * W : (rel + 1) * W] = t.astype(BF16)
        c_t[p] = send(tsnd, chunk(trcv2, trcv1, p), sibling)
        for rel in range(4):
            t = dot_nn(hbuf[0:m, :], dn[:, pl.ds(col(rel, c), W)])
            town[:, rel * W : (rel + 1) * W] = t.astype(BF16)

    s_ret = {}
    l_ret = {}

    def give_back(p):
        town, rt = chunk(town2, town1, p), chunk(rt2, rt1, p)
        trcv = chunk(trcv2, trcv1, p)
        c_t[p].wait_recv()
        for half in (1, 0):
            cols = slice(2 * half * W, 2 * (half + 1) * W)
            window = pl.ds(2 * half * W, 2 * W)
            town[:, cols] = (town[:, cols].astype(F32) + trcv[:, cols].astype(F32)).astype(BF16)
            s_ret[p, half] = group()
            for k in (2, 1, 3):
                send(
                    town.at[owner_rows(k, p), window], rt.at[owner_rows(0, p), window],
                    dev(xx=at_x(k)), s_ret[p, half],
                )
        l_ret[p] = local(town.at[owner_rows(0, p)], rt.at[owner_rows(0, p)])

    c_y = {}

    def combine(p):
        wm, rt = chunk(wmat2, wmat1, p), chunk(rt2, rt1, p)
        l_ret[p].wait()
        for rel in (2, 3, 1, 0):
            if rel in (1, 2):
                half = rel // 2
                arrived(s_ret[p, half], rt.at[pl.ds(0, 3 * per_owner(p)), pl.ds(2 * half * W, 2 * W)])
            order = list(enumerate(BLOCKS[p]))
            for i, k in order if rel in (2, 1) else order[::-1]:
                got = dot_nn(wm[i * T : (i + 1) * T, :], rt[:, rel * W : (rel + 1) * W])
                if k == 0:
                    got = got + sh_own[rel] + sh_r[rel].astype(F32)
                if rel < 2:
                    pb[k, rel] = got
                elif rel == 2:
                    ysnd[k, 0] = got.astype(BF16)
                    c_y[k, 1] = send(ysnd.at[k, 0], yrcv.at[k, 1], y_up)
                else:
                    ysnd[k, 1] = got.astype(BF16)
                    c_y[k, 0] = send(ysnd.at[k, 1], yrcv.at[k, 0], y_down)

    def wait_y(p):
        k = BLOCKS[p][0]
        arrived(s_yfw[p], nb.at[k] if p < 4 else nb.at[k, pl.ds(0, 2)])

    slots(0, 0)
    for rel in (3, 2):
        normalise(rel)
    c_sib = send(nb.at[0], nsib, sibling)
    slots(0, 1)
    arrived(s_code, cz.at[pl.ds(1, NZ - 1)])
    for p in (1, 2, 3, 4):
        build_slots(p)
    l_router.wait()
    c_sib.wait_recv()
    logits = None
    for rel in range(4):
        t = dot_nt(router[:, pl.ds(col(rel, c), W)], nb[0, rel])
        t = t + dot_nt(router[:, pl.ds(col(rel, sc), W)], nsib[rel])
        logits = t if logits is None else logits + t
    scores = jnp.where(chosen, 1.0 / (1.0 + jnp.exp(-logits)), 0.0)
    gates = scores / jnp.sum(scores, axis=0, keepdims=True) * SCALE
    gates = jnp.where(alive, gates, 0.0).astype(BF16)
    sel_r = lax.broadcasted_iota(jnp.int32, (experts, experts), 0)
    sel_c = lax.broadcasted_iota(jnp.int32, (experts, experts), 1)
    sel_w = 2 * ((sel_r & 3) * NZ + (sel_r >> 3)) + ((sel_r >> 2) & 1)
    gt[...] = dot_nn(jnp.where(sel_c == sel_w, 1.0, 0.0).astype(BF16), gates)
    s_gate = group()
    for k in range(1, NZ):
        send(gt.at[pl.ds(pl.multiple_of(at_z(k) * 8, 8), 8)], gz.at[k], dev(zz=at_z(k)), s_gate)
    gz[0] = gt[pl.ds(pl.multiple_of(z * 8, 8), 8), :]

    ring_step(0)
    slots(1, 0)
    forward(0)
    l_sg.wait()
    l_su.wait()
    l_sd.wait()
    swiglu(T, lambda rel: nb[0, rel], lambda rel: nsib[rel], sgu)
    wait_y(1)
    slots(1, 1)
    ring_step(1)
    slots(2, 0)
    for rel in range(4):
        sh_s[rel] = dot_nn(hbuf[0:T, :], sdn[:, pl.ds(col(rel, sc), W)]).astype(BF16)
    c_sh = send(sh_s, sh_r, sibling)
    for rel in range(4):
        sh_own[rel] = dot_nn(hbuf[0:T, :], sdn[:, pl.ds(col(rel, c), W)])
    l_g.wait()
    l_u.wait()
    l_d.wait()
    expert(0)
    wait_y(2)
    slots(2, 1)
    ring_step(2)
    slots(3, 0)
    forward(1)
    ring_step(3)
    wait_y(3)
    slots(3, 1)
    wait_y(4)
    slots(4, 0)
    slots(4, 1)
    give_back(0)
    expert(1)
    forward(2)
    arrived(s_gate, gz.at[pl.ds(1, NZ - 1)])
    for p in range(5):
        build_weights(p)
    expert(2)
    forward(3)
    expert(3)
    forward(4)
    expert(4)
    give_back(4)
    give_back(3)
    give_back(2)
    give_back(1)
    c_sh.wait_recv()
    combine(0)

    back = {}

    def value(k, ch):
        c_y[k, ch].wait_recv()
        return pb[k, ch] + yrcv[k, ch].astype(F32)

    def pass_on(wi, way, s, ch, k, to):
        v = value(k, ch)
        if (way, s - 1, ch) in back:
            back[way, s - 1, ch].wait_recv()
            v = v + rs_r[wi, s - 1, ch].astype(F32)
        rs_s[wi, s, ch] = v.astype(BF16)
        back[way, s, ch] = send(rs_s.at[wi, s, ch], rs_r.at[wi, s, ch], to)

    combine(4)
    pass_on(0, "L", 0, 0, 4, z_left)
    pass_on(1, "R", 0, 1, 4, z_right)
    for s in (1, 2, 3):
        combine(4 - s)
        for ch in (1, 0):
            pass_on(0, "L", s, ch, 4 - s, z_left)
            pass_on(1, "R", s, 1 - ch if s < 3 else ch, 4 + s, z_right)

    def finish(ch):
        v = value(0, ch)
        for wi, way in ((0, "L"), (1, "R")):
            back[way, 3, ch].wait_recv()
            v = v + rs_r[wi, 3, ch].astype(F32)
        return v

    fb_s[...] = finish(1).astype(BF16)
    c_fb = send(fb_s, fb_r, y_up)
    mine = finish(0) + st[0].astype(F32)
    c_fb.wait_recv()
    nxt = (mine + fb_r[...].astype(F32)).astype(BF16)
    wide = nxt.astype(F32)
    out_s[...] = wide
    q_s[...] = squares(wide)
    inv2 = inverse(share(q_s, q_r), q_s, q_r)
    out_n[...] = inv2 * gain_row(ngain, 0)
    for cp in copies[-N_SEND:]:
        cp.wait_send()


N_SEND = 32
N_RECV = 94


def on_device(
    attn_out, out_proj, residual, norm_gain, router, expert_gate_up, expert_down,
    shared_gate_up, shared_down, routes, live_rows, next_gain,
):
    T, W = attn_out.shape
    D = out_proj.shape[1]
    FF = expert_down.shape[1]
    FFP = -(-FF // 128) * 128
    H = D // 2
    R2, R1 = NX * 2 * CAP, NX * CAP_PAD
    fanout = routes.shape[1]
    vm = pltpu.VMEM
    both = [vm((3, R2, H), BF16), vm((2, R1, H), BF16)]
    scratch = [
        vm((T, W), BF16), vm((W, D), BF16), vm((T, W), BF16), vm((D,), F32), vm((8, W), F32), vm((64, D), BF16),
        vm((2 * FFP, D), BF16), vm((FFP, D), BF16), vm((2 * FFP, D), BF16), vm((FFP, D), BF16),
        vm((fanout, T), jnp.int32), vm((D,), F32), vm((8, W), F32),
        vm((4, T, W), BF16), vm((4, T, W), BF16), vm((3, T, W), BF16), vm((3, T, W), BF16),
        vm((4, T, W), BF16), vm((T, W), F32), vm((8, T), F32), vm((7, 8, T), F32),
        vm((64, T), F32), vm((NZ, 8, T), F32), vm((64, T), F32), vm((NZ, 8, T), F32),
        vm((NZ, 4, T, W), BF16), vm((4, T, W), BF16),
        vm((3, R2, 2 * T), BF16), vm((2, R1, T), BF16), vm((3, 2 * T, R2), BF16), vm((2, T, R1), BF16),
        *both, *both, *both,
        vm((R2, 2 * FFP), F32), vm((R2, FFP), BF16),
        *both, *both, *both, *both,
        vm((4, T, W), F32), vm((4, T, W), BF16), vm((4, T, W), BF16),
        vm((NZ, 2, T, W), F32), vm((NZ, 2, T, W), BF16), vm((NZ, 2, T, W), BF16),
        vm((2, 4, 2, T, W), BF16), vm((2, 4, 2, T, W), BF16),
        vm((T, W), BF16), vm((T, W), BF16), vm((8, T), F32), vm((7, 8, T), F32),
        pltpu.SemaphoreType.DMA((13,)), pltpu.SemaphoreType.DMA((10,)),
        pltpu.SemaphoreType.DMA((N_SEND,)), pltpu.SemaphoreType.DMA((N_RECV,)),
    ]
    hbm = pl.BlockSpec(memory_space=pl.ANY)
    stream, scale = pl.pallas_call(
        kernel,
        out_shape=(jax.ShapeDtypeStruct((T, W), F32), jax.ShapeDtypeStruct((T, W), F32)),
        in_specs=[pl.BlockSpec(memory_space=pltpu.SMEM)] + [hbm] * 11,
        out_specs=(pl.BlockSpec(memory_space=pltpu.VMEM), pl.BlockSpec(memory_space=pltpu.VMEM)),
        scratch_shapes=scratch,
        compiler_params=pltpu.CompilerParams(
            collective_id=0, has_side_effects=True, vmem_limit_bytes=67043328
        ),
    )(
        live_rows, attn_out, out_proj, residual, norm_gain, router.T, expert_gate_up,
        expert_down, shared_gate_up, shared_down, routes.T, next_gain,
    )
    return stream.astype(BF16), (stream * scale).astype(BF16)


def solution(mesh):
    in_specs = (
        P("ep", "tp"),
        P("tp", None),
        P("ep", None),
        P(),
        P(),
        P(("ep", "tp"), None, None, None),
        P(("ep", "tp"), None, None),
        P(None, "tp", None),
        P("tp", None),
        P("ep", None),
        P("ep"),
        P(),
    )
    out_specs = (P("ep", "tp"), P("ep", "tp"))
    return jax.shard_map(
        on_device, mesh=mesh, in_specs=in_specs, out_specs=out_specs, check_vma=False
    )
```
